32 devices in a mesh: groups: 2 (over y), ep: 8 (over z, x), tp: 2 (over core).
Axes of the slice: x: 2, y: 2, z: 4, core: 2. Of those that a mesh axis runs over, the one named last changes fastest.
Arguments:
- hidden: bfloat16 [128, 4096], P(('groups', 'ep', 'tp')), parts along dimension 0, may hold values from -6 to 6
- norm_gain: float32 [4096], replicated, may hold values from 0.5 to 1.5
- rot_left: float32 [64, 64], replicated, may hold values from -0.75 to 0.75
- rot_right: float32 [64, 64], replicated, may hold values from -0.75 to 0.75
- expert_ids: int32 [128, 8], P(('groups', 'ep')), parts along dimension 0, may hold values from 0 to 63, as said below
- gate_weights: float32 [128, 8], P(('groups', 'ep')), parts along dimension 0, may hold values from 0.05 to 1
- w_gate: bfloat16 [128, 4096, 384], P('ep', 'tp'), may hold values from -0.09375 to 0.09375
- w_up: bfloat16 [128, 4096, 384], P('ep', 'tp'), may hold values from -0.09375 to 0.09375
- w_down: bfloat16 [128, 384, 4096], P('ep', None, 'tp'), may hold values from -0.21875 to 0.21875
- unit_scales: float32 [128, 2, 384], P('ep'), may hold values from 0.25 to 1.75
Outputs:
- moe_out: bfloat16 [128, 4096], P(('groups', 'ep', 'tp')), parts along dimension 0
The draws below stay inside these ranges and needn't reach their ends.
There are 2 independent parts, one for each index of `groups`. The reference program is written for one: setup_inputs(seed, part) draws one part's arguments, and reference() takes and returns one part's arrays. A program takes and returns all parts, laid end to end along the dimension named above; an argument that names none is the same for every part. Nothing has to cross between parts.
Inputs may be any that keep to these rules, and one draw needn't show every extreme that they name: `expert_ids`: each row names 8 different experts. In each aligned block of 8 rows (the rows of one index of ep) no expert is named by more than 2 rows, and in every block some experts are named by exactly 2 rows; every expert is named by exactly 2 rows in some block.
All inputs are finite; a program needn't handle non-finite values.
Results may differ from the reference program's by a relative error of at most 0.0082.
Values may be sent and summed in bfloat16 or wider, within the bound.
No kernel may reach another device: no remote copies, remote signals or barrier semaphores. Data moves between devices by JAX's collectives and lax.ppermute only.
A program may use at most 128 MiB of HBM per device.

```python
import math
import jax
import jax.numpy as jnp
from jax import lax

D = 4096
ROT = 64
FF = 768
EXPERTS = 64
TOPK = 8
R_DEV = 4
ROWS = 64
CAP = 2
N_TP = 2


def draw_expert_ids(key, part):
    group_rows = R_DEV * N_TP
    block_count = ROWS // group_rows
    labels = jax.random.permutation(jax.random.fold_in(key, 11), EXPERTS).astype(jnp.int32)
    offset = jax.random.randint(jax.random.fold_in(key, 12), (), 0, EXPERTS, dtype=jnp.int32)
    block_index = jnp.arange(block_count, dtype=jnp.int32)[:, None, None]
    row_index = jnp.arange(group_rows, dtype=jnp.int32)[None, :, None]
    choice_index = jnp.arange(TOPK, dtype=jnp.int32)[None, None, :]
    spot = (block_index * TOPK + row_index // CAP * TOPK + choice_index + offset) % EXPERTS
    chosen = labels[spot]

    def order_of(block):
        return jax.random.permutation(jax.random.fold_in(key, 1000 + block), group_rows).astype(jnp.int32)
    orders = jax.vmap(order_of)(jnp.arange(block_count, dtype=jnp.int32))
    chosen = jnp.take_along_axis(chosen, orders[:, :, None], axis=1)
    return chosen.reshape(ROWS, TOPK).astype(jnp.int32)


def block_levels(stream_key, extent, shards, low, high):
    level = 1.0
    for dim, parts in shards:
        heights = jax.random.uniform(jax.random.fold_in(jax.random.fold_in(stream_key, 6), dim), (parts,), jnp.float32, low / len(shards), high / len(shards))
        level = level * jnp.repeat(jnp.exp(heights), extent[dim] // parts).reshape((-1,) + (1,) * (len(extent) - 1 - dim))
    return level


def gaussian(rng, shape, width, limit, shards=(), kind=jnp.bfloat16):
    entries = jax.random.normal(rng, shape, jnp.float32) * width
    if len(shards) > 0:
        entries = block_levels(rng, shape, shards, -0.22, 0.18) * entries
    return jnp.clip(entries, min=-limit, max=limit).astype(kind)


def setup_inputs(seed: int = 0, part: int = 0) -> dict:
    keys = jax.random.split(jax.random.key(seed), 11)
    part_splits = jax.random.split(jax.random.fold_in(keys[10], part), 11)
    hidden = gaussian(part_splits[0], (ROWS, D), 1.0, 6.0, ((0, 16),))
    norm_gain = jnp.clip(1.0 + 0.1 * jax.random.normal(keys[1], (D,), jnp.float32), 0.5, 1.5)
    rot_left = gaussian(keys[2], (ROT, ROT), ROT ** -0.5, 0.75, (), jnp.float32)
    rot_right = gaussian(keys[3], (ROT, ROT), ROT ** -0.5, 0.75, (), jnp.float32)
    expert_ids = draw_expert_ids(jax.random.fold_in(jax.random.fold_in(keys[10], part), 71), part)
    gate_weights = jnp.clip(jnp.exp(math.log(1.0) - 2.9957323 * jax.random.uniform(part_splits[5], (ROWS, TOPK), jnp.float32) ** block_levels(part_splits[5], (ROWS, TOPK), ((0, 8),), -0.2, 0.2)), 0.05, 1.0)
    w_gate = gaussian(keys[6], (2 * EXPERTS, D, FF // 2), D ** -0.5, 0.09375, ((0, 8), (1, 2)))
    w_up = gaussian(keys[7], (2 * EXPERTS, D, FF // 2), D ** -0.5, 0.09375, ((0, 8), (1, 2)))
    w_down = gaussian(keys[8], (2 * EXPERTS, FF // 2, D), FF ** -0.5, 0.21875, ((0, 8), (2, 2)))
    unit_scales = jnp.clip(1.0 + 0.15 * jax.random.normal(keys[9], (2 * EXPERTS, 2, FF // 2), jnp.float32), 0.25, 1.75)
    return {"hidden": hidden, "norm_gain": norm_gain, "rot_left": rot_left, "rot_right": rot_right, "expert_ids": expert_ids, "gate_weights": gate_weights, "w_gate": w_gate, "w_up": w_up, "w_down": w_down, "unit_scales": unit_scales}


def rotate(hidden, norm_gain, rot_left, rot_right):
    values = hidden.astype(jnp.float32)
    mean_square = lax.optimization_barrier(jnp.mean(values * values, axis=1, keepdims=True))
    normed = values * lax.rsqrt(mean_square + 1e-06) * norm_gain[None, :]
    factor = rot_left.shape[0]
    square = normed.reshape(-1, factor, factor)
    turned = jnp.einsum('ij,rjk->rik', rot_left, square, precision=lax.Precision.HIGHEST)
    turned = jnp.einsum('rik,lk->ril', turned, rot_right, precision=lax.Precision.HIGHEST)
    return turned.reshape(normed.shape).astype(jnp.bfloat16)

def reference(hidden, norm_gain, rot_left, rot_right, expert_ids, gate_weights, w_gate, w_up, w_down, unit_scales):
    row_count = hidden.shape[0]
    group_rows = R_DEV * N_TP
    block_count = row_count // group_rows
    half_ff = w_gate.shape[2]
    rotated = rotate(hidden, norm_gain, rot_left, rot_right)
    weight_norm = (gate_weights / lax.optimization_barrier(jnp.sum(gate_weights, axis=1, keepdims=True))).astype(jnp.bfloat16)
    blocks = expert_ids.reshape(block_count, group_rows * TOPK)
    onehot = (blocks[:, :, None] == jnp.arange(EXPERTS, dtype=jnp.int32)[None, None, :]).astype(jnp.int32)
    slot_rank = lax.optimization_barrier(jnp.sum((jnp.cumsum(onehot, axis=1) - onehot) * onehot, axis=2))
    position = (jnp.arange(block_count, dtype=jnp.int32)[:, None] * group_rows + jnp.arange(group_rows * TOPK, dtype=jnp.int32)[None, :] // TOPK).astype(jnp.int32)
    weight_flat = weight_norm.astype(jnp.float32).reshape(block_count, group_rows * TOPK)
    slot_index = jnp.arange(CAP, dtype=jnp.int32)

    def expert_step(total, expert):
        selects = ((blocks == expert)[:, :, None] & (slot_rank[:, :, None] == slot_index[None, None, :])).astype(jnp.int32)
        gather_index = lax.optimization_barrier(jnp.sum(selects * position[:, :, None], axis=1)).reshape(-1).astype(jnp.int32)
        portion = lax.optimization_barrier(jnp.sum(selects.astype(jnp.float32) * weight_flat[:, :, None], axis=1)).reshape(-1)
        inputs = jnp.take(rotated, gather_index, axis=0)
        gate_full = jnp.concatenate((w_gate[expert], w_gate[EXPERTS + expert]), axis=1)
        up_full = jnp.concatenate((w_up[expert], w_up[EXPERTS + expert]), axis=1)
        gate_scale = jnp.concatenate((unit_scales[expert, 0], unit_scales[EXPERTS + expert, 0]), axis=0)
        up_scale = jnp.concatenate((unit_scales[expert, 1], unit_scales[EXPERTS + expert, 1]), axis=0)
        gate_sum = jnp.dot(inputs, gate_full, preferred_element_type=jnp.float32) * gate_scale[None, :]
        up_sum = jnp.dot(inputs, up_full, preferred_element_type=jnp.float32) * up_scale[None, :]
        hidden_units = (jax.nn.silu(gate_sum) * up_sum).astype(jnp.bfloat16)
        lower_out = jnp.dot(hidden_units[:, :half_ff], w_down[expert], preferred_element_type=jnp.float32).astype(jnp.bfloat16)
        upper_out = jnp.dot(hidden_units[:, half_ff:], w_down[EXPERTS + expert], preferred_element_type=jnp.float32).astype(jnp.bfloat16)
        expert_out = lax.optimization_barrier((lower_out.astype(jnp.float32) + upper_out.astype(jnp.float32)).astype(jnp.bfloat16))
        contribution = portion[:, None] * expert_out.astype(jnp.float32)
        return (total.at[gather_index].add(contribution), None)
    start = jnp.zeros((row_count, hidden.shape[1]), jnp.float32)
    total, _ = lax.scan(expert_step, start, jnp.arange(EXPERTS, dtype=jnp.int32))
    return total.astype(jnp.bfloat16)
```

```python
import jax
import jax.numpy as jnp
from jax import lax
from jax.sharding import PartitionSpec as P

META = 128


def rotate(hidden, norm_gain, rot_left, rot_right):
    values = hidden.astype(jnp.float32)
    mean_square = jnp.mean(values * values, axis=1, keepdims=True)
    normed = values * lax.rsqrt(mean_square + 1e-06) * norm_gain[None, :]
    factor = rot_left.shape[0]
    square = normed.reshape(-1, factor, factor)
    turned = jnp.einsum("ij,rjk->rik", rot_left, square, precision=lax.Precision.HIGHEST)
    turned = jnp.einsum("rik,lk->ril", turned, rot_right, precision=lax.Precision.HIGHEST)
    return turned.reshape(normed.shape).astype(jnp.bfloat16)


def body(
    hidden,
    norm_gain,
    rot_left,
    rot_right,
    expert_ids,
    gate_weights,
    w_gate,
    w_up,
    w_down,
    unit_scales,
):
    ep_count = lax.axis_size("ep")
    tp_count = lax.axis_size("tp")
    tp_index = lax.axis_index("tp")
    peers = ep_count * tp_count
    own_rows, width = hidden.shape
    part_width = width // tp_count
    group_rows, top_count = expert_ids.shape
    held_halves, _, half_ff = w_gate.shape
    experts = held_halves * ep_count // 2
    capacity = 5 * group_rows * top_count // (2 * experts)
    slots = capacity * ep_count
    all_rows = peers * own_rows

    rotated = rotate(hidden, norm_gain, rot_left, rot_right)
    weight_norm = (gate_weights / jnp.sum(gate_weights, axis=1, keepdims=True)).astype(jnp.bfloat16)
    meta = jnp.concatenate((expert_ids.astype(jnp.bfloat16), weight_norm), axis=1)
    meta = lax.dynamic_slice_in_dim(meta, tp_index * own_rows, own_rows, axis=0)
    meta = jnp.pad(meta, ((0, 0), (0, META - 2 * top_count)))
    halves = rotated.reshape(own_rows, tp_count, part_width).transpose(1, 0, 2)
    halves = jnp.concatenate(
        (halves, jnp.broadcast_to(meta[None], (tp_count, own_rows, META))), axis=2
    )
    outgoing = jnp.broadcast_to(halves[None], (ep_count,) + halves.shape)
    outgoing = outgoing.reshape(peers, own_rows, part_width + META)
    received = lax.all_to_all(outgoing, ("ep", "tp"), split_axis=0, concat_axis=0, tiled=True)
    received = received.reshape(all_rows, part_width + META)
    rows = received[:, :part_width]
    row_ids = received[:, part_width : part_width + top_count].astype(jnp.int32)
    row_weights = received[:, part_width + top_count : part_width + 2 * top_count].astype(
        jnp.float32
    )

    held = (
        lax.axis_index("ep") * held_halves + jnp.arange(held_halves, dtype=jnp.int32)
    ) % experts
    named = row_ids.T[None, :, :] == held[:, None, None]
    member = jnp.sum(named.astype(jnp.float32), axis=1)
    weight = jnp.sum(jnp.where(named, row_weights.T[None, :, :], 0.0), axis=1)
    rank = jnp.cumsum(member, axis=1) - member
    slot_index = jnp.arange(slots, dtype=jnp.float32)[None, :, None]
    select = (member[:, None, :] > 0) & (rank[:, None, :] == slot_index)
    spread = jnp.where(select, weight[:, None, :], 0.0).astype(jnp.bfloat16)
    inputs = jnp.dot(
        select.astype(jnp.bfloat16).reshape(held_halves * slots, all_rows),
        rows,
        preferred_element_type=jnp.float32,
    ).astype(jnp.bfloat16)
    inputs = inputs.reshape(held_halves, slots, part_width)
    gate_part = jnp.einsum("hsd,hdf->hsf", inputs, w_gate, preferred_element_type=jnp.float32)
    up_part = jnp.einsum("hsd,hdf->hsf", inputs, w_up, preferred_element_type=jnp.float32)
    swap = [(i, i ^ 1) for i in range(tp_count)]
    gate_other = lax.ppermute(gate_part.astype(jnp.bfloat16), "tp", swap)
    up_other = lax.ppermute(up_part.astype(jnp.bfloat16), "tp", swap)
    gate_sum = (gate_part + gate_other.astype(jnp.float32)) * unit_scales[:, 0, None, :]
    up_sum = (up_part + up_other.astype(jnp.float32)) * unit_scales[:, 1, None, :]
    units = (jax.nn.silu(gate_sum) * up_sum).astype(jnp.bfloat16)
    down = jnp.einsum("hsf,hfd->hsd", units, w_down, preferred_element_type=jnp.float32)
    down = down.astype(jnp.bfloat16).reshape(held_halves * slots, part_width)
    combined = lax.dot_general(
        spread.reshape(held_halves * slots, all_rows),
        down,
        (((0,), (0,)), ((), ())),
        preferred_element_type=jnp.float32,
    ).astype(jnp.bfloat16)
    returned = lax.all_to_all(
        combined.reshape(peers, own_rows, part_width),
        ("ep", "tp"),
        split_axis=0,
        concat_axis=0,
        tiled=True,
    )
    returned = returned.reshape(ep_count, tp_count, own_rows, part_width)
    total = jnp.sum(returned.astype(jnp.float32), axis=0)
    return total.transpose(1, 0, 2).reshape(own_rows, width).astype(jnp.bfloat16)


def solution(mesh):
    placed = (
        P(("groups", "ep", "tp"), None),
        P(),
        P(),
        P(),
        P(("groups", "ep"), None),
        P(("groups", "ep"), None),
        P("ep", "tp", None),
        P("ep", "tp", None),
        P("ep", None, "tp"),
        P("ep", None, None),
    )
    return jax.shard_map(
        body, mesh=mesh, in_specs=placed, out_specs=P(("groups", "ep", "tp"), None), check_vma=False
    )
```

```python
import functools

import jax
import jax.numpy as jnp
from jax import lax
from jax.experimental import pallas as pl
from jax.experimental.pallas import tpu as pltpu
from jax.sharding import PartitionSpec as P

LANES = 128
META = 128
MIB = 1 << 20


def exact_dot(left, right):
    return jnp.dot(
        left, right, precision=lax.Precision.HIGHEST, preferred_element_type=jnp.float32
    )


def prelude_kernel(held_halves, experts, ep_count, tp_count, *refs):
    given, out, held, sems = refs[:6], refs[6], refs[7:13], refs[13]
    copies = [pltpu.make_async_copy(a, b, sems.at[i]) for i, (a, b) in enumerate(zip(given, held))]
    for copy in copies:
        copy.start()
    for copy in copies:
        copy.wait()
    hidden, norm_gain, rot_left, rot_right, ids, weights = held
    own_rows, width = hidden.shape
    factor = rot_left.shape[0]
    tiles = width // LANES
    pack = LANES // factor
    top_count = ids.shape[1]
    values = hidden[...].astype(jnp.float32)
    mean_square = jnp.sum(values * values, axis=1, keepdims=True) / width
    normed = values * lax.rsqrt(mean_square + 1e-06) * norm_gain[...]
    lines = jnp.concatenate(
        [normed[:, t * LANES : (t + 1) * LANES] for t in range(tiles)], axis=0
    )
    right = rot_right[...]
    two = jnp.concatenate([right] * pack, axis=0)
    two = jnp.concatenate([two] * pack, axis=1)
    square = (LANES, LANES)
    line = lax.broadcasted_iota(jnp.int32, square, 0)
    lane = lax.broadcasted_iota(jnp.int32, square, 1)
    two = jnp.where(line // factor == lane // factor, two, 0.0)
    lines = lax.dot_general(
        lines,
        two,
        (((1,), (1,)), ((), ())),
        precision=lax.Precision.HIGHEST,
        preferred_element_type=jnp.float32,
    )
    count = tiles * own_rows
    tall = (count, factor)
    tile_of = lax.broadcasted_iota(jnp.int32, tall, 0) // own_rows
    column = lax.broadcasted_iota(jnp.int32, tall, 1)
    picks = [jnp.where(column == pack * tile_of + p, 1.0, 0.0) for p in range(pack)]
    same_row = (
        lax.broadcasted_iota(jnp.int32, (count, count), 0) % own_rows
        == lax.broadcasted_iota(jnp.int32, (count, count), 1) % own_rows
    )
    chosen = exact_dot(jnp.concatenate(picks, axis=0), rot_left[...])
    turned = jnp.zeros((count, LANES), jnp.float32)
    for p_in in range(pack):
        wide = lax.dot_general(
            chosen,
            picks[p_in],
            (((1,), (1,)), ((), ())),
            precision=lax.Precision.HIGHEST,
            preferred_element_type=jnp.float32,
        )
        for p_out in range(pack):
            block = jnp.where(same_row, wide[p_out * count : (p_out + 1) * count, :], 0.0)
            value = exact_dot(block, lines)
            shift = ((p_out - p_in) * factor) % LANES
            if shift:
                value = pltpu.roll(value, shift, 1)
            turned = turned + jnp.where(
                lax.broadcasted_iota(jnp.int32, (count, LANES), 1) // factor == p_out, value, 0.0
            )
    rotated = jnp.concatenate(
        [turned[t * own_rows : (t + 1) * own_rows, :] for t in range(tiles)], axis=1
    ).astype(jnp.bfloat16)

    gate_weights = weights[...]
    share = (gate_weights / jnp.sum(gate_weights, axis=1, keepdims=True)).astype(jnp.bfloat16)
    both = jnp.concatenate((ids[...].astype(jnp.float32), share.astype(jnp.float32)), axis=1)
    meta = jnp.concatenate(
        [both[t * own_rows : (t + 1) * own_rows, :] for t in range(tp_count)]
        + [jnp.zeros((own_rows, META - 2 * top_count * tp_count), jnp.float32)],
        axis=1,
    )
    spot = lax.broadcasted_iota(jnp.int32, meta.shape, 1) == META - 1
    part_width = width // tp_count
    for e in range(ep_count):
        first = float(e * held_halves % experts)
        tail = jnp.where(spot, first, meta).astype(jnp.bfloat16)
        for t in range(tp_count):
            out[e * tp_count + t, :, :part_width] = rotated[
                :, t * part_width : (t + 1) * part_width
            ]
            out[e * tp_count + t, :, part_width:] = tail


def gate_up_kernel(
    tp_count, top_count, slots, received_ref, w_gate, w_up, part, to_send, spread, inputs
):
    held_halves, part_width, half_ff = w_gate.shape
    peers, own_rows, _ = received_ref.shape
    all_rows = peers * own_rows
    received = received_ref[...].reshape(all_rows, part_width + META)
    meta = received[:, part_width:].astype(jnp.float32).T
    shape = (held_halves, all_rows)
    held = lax.broadcasted_iota(jnp.int32, shape, 0).astype(jnp.float32) + meta[META - 1 :, :]
    group = 2 * top_count
    sender = lax.broadcasted_iota(jnp.int32, (group, all_rows), 1) // own_rows % tp_count
    chosen = meta[:group, :]
    for t in range(1, tp_count):
        chosen = jnp.where(sender == t, meta[t * group : (t + 1) * group, :], chosen)
    member = jnp.zeros(shape, jnp.float32)
    weight = jnp.zeros(shape, jnp.float32)
    for choice in range(top_count):
        named = chosen[choice : choice + 1, :] == held
        member = jnp.where(named, 1.0, member)
        weight = jnp.where(named, chosen[top_count + choice : top_count + choice + 1, :], weight)
    square = (all_rows, all_rows)
    earlier = lax.broadcasted_iota(jnp.int32, square, 0) < lax.broadcasted_iota(
        jnp.int32, square, 1
    )
    rank = jnp.dot(
        member.astype(jnp.bfloat16),
        jnp.where(earlier, 1.0, 0.0).astype(jnp.bfloat16),
        preferred_element_type=jnp.float32,
    )
    rank = jnp.where(member > 0, rank, -1.0)
    slot_index = lax.broadcasted_iota(jnp.int32, (slots, all_rows), 0).astype(jnp.float32)
    selects = []
    for j in range(held_halves):
        select = rank[j : j + 1, :] == slot_index
        selects.append(jnp.where(select, 1.0, 0.0))
        spread[j * slots : (j + 1) * slots, :] = jnp.where(
            select, weight[j : j + 1, :], 0.0
        ).astype(jnp.bfloat16)
    select = jnp.concatenate(selects, axis=0).astype(jnp.bfloat16)
    inputs[...] = jnp.dot(
        select, received[:, :part_width], preferred_element_type=jnp.float32
    ).astype(jnp.bfloat16)
    for j in range(held_halves):
        window = slice(j * slots, (j + 1) * slots)
        rows = inputs[window, :]
        for index, w in enumerate((w_gate, w_up)):
            value = jnp.dot(rows, w[j], preferred_element_type=jnp.float32)
            part[index, window, :] = value
            to_send[index, window, :] = value.astype(jnp.bfloat16)


def down_kernel(slots, part, other, unit_scales, spread, w_down, out, held, lines, sems):
    held_halves = w_down.shape[0]
    copies = [
        pltpu.make_async_copy(w_down.at[j], held.at[j], sems.at[j]) for j in range(held_halves)
    ]
    for copy in copies:
        copy.start()
    for j in range(held_halves):
        window = slice(j * slots, (j + 1) * slots)
        gate = (part[0, window, :] + other[0, window, :].astype(jnp.float32)) * unit_scales[
            j, 0:1, :
        ]
        up = (part[1, window, :] + other[1, window, :].astype(jnp.float32)) * unit_scales[
            j, 1:2, :
        ]
        units = (gate / (1.0 + jnp.exp(-gate)) * up).astype(jnp.bfloat16)
        copies[j].wait()
        lines[window, :] = jnp.dot(
            units, held[j], preferred_element_type=jnp.float32
        ).astype(jnp.bfloat16)
    out[...] = lax.dot_general(
        spread[...], lines[...], (((0,), (0,)), ((), ())), preferred_element_type=jnp.float32
    ).astype(jnp.bfloat16)


def body(
    hidden,
    norm_gain,
    rot_left,
    rot_right,
    expert_ids,
    gate_weights,
    w_gate,
    w_up,
    w_down,
    unit_scales,
):
    ep_count = lax.axis_size("ep")
    tp_count = lax.axis_size("tp")
    peers = ep_count * tp_count
    own_rows, width = hidden.shape
    part_width = width // tp_count
    group_rows, top_count = expert_ids.shape
    held_halves, _, half_ff = w_gate.shape
    experts = held_halves * ep_count // 2
    capacity = 5 * group_rows * top_count // (2 * experts)
    slots = capacity * ep_count
    all_rows = peers * own_rows
    lines = held_halves * slots

    vmem = pl.BlockSpec(memory_space=pltpu.VMEM)
    given = (hidden, norm_gain[None, :], rot_left, rot_right, expert_ids, gate_weights)
    outgoing = pl.pallas_call(
        functools.partial(prelude_kernel, held_halves, experts, ep_count, tp_count),
        out_shape=pltpu.VMEM((peers, own_rows, part_width + META), jnp.bfloat16),
        in_specs=[pl.BlockSpec(memory_space=pltpu.HBM)] * len(given),
        out_specs=vmem,
        scratch_shapes=[pltpu.VMEM(array.shape, array.dtype) for array in given]
        + [pltpu.SemaphoreType.DMA((len(given),))],
        cost_estimate=pl.CostEstimate(flops=1 << 36, bytes_accessed=MIB, transcendentals=0),
        compiler_params=pltpu.CompilerParams(vmem_limit_bytes=4 * MIB),
        name="prelude",
    )(*[pltpu.with_memory_space_constraint(array, pltpu.HBM) for array in given])
    received = lax.all_to_all(outgoing, ("ep", "tp"), split_axis=0, concat_axis=0, tiled=True)
    part, to_send, spread = pl.pallas_call(
        functools.partial(gate_up_kernel, tp_count, top_count, slots),
        out_shape=(
            pltpu.VMEM((2, lines, half_ff), jnp.float32),
            pltpu.VMEM((2, lines, half_ff), jnp.bfloat16),
            pltpu.VMEM((lines, all_rows), jnp.bfloat16),
        ),
        in_specs=[vmem] * 3,
        out_specs=(vmem,) * 3,
        scratch_shapes=[pltpu.VMEM((lines, part_width), jnp.bfloat16)],
        compiler_params=pltpu.CompilerParams(vmem_limit_bytes=5 * MIB),
        name="gate_up",
    )(
        received,
        pltpu.with_memory_space_constraint(w_gate, pltpu.VMEM),
        pltpu.with_memory_space_constraint(w_up, pltpu.VMEM),
    )
    other = lax.ppermute(to_send, "tp", [(i, i ^ 1) for i in range(tp_count)])
    combined = pl.pallas_call(
        functools.partial(down_kernel, slots),
        out_shape=jax.ShapeDtypeStruct((all_rows, part_width), jnp.bfloat16),
        in_specs=[vmem] * 4 + [pl.BlockSpec(memory_space=pltpu.HBM)],
        out_specs=vmem,
        scratch_shapes=[
            pltpu.VMEM(w_down.shape, w_down.dtype),
            pltpu.VMEM((lines, part_width), jnp.bfloat16),
            pltpu.SemaphoreType.DMA((held_halves,)),
        ],
        compiler_params=pltpu.CompilerParams(vmem_limit_bytes=36 * MIB),
        name="down",
    )(part, other, unit_scales, spread, w_down)
    returned = lax.all_to_all(
        combined.reshape(peers, own_rows, part_width),
        ("ep", "tp"),
        split_axis=0,
        concat_axis=0,
        tiled=True,
    )
    returned = returned.reshape(ep_count, tp_count, own_rows, part_width)
    total = jnp.sum(returned.astype(jnp.float32), axis=0)
    return total.transpose(1, 0, 2).reshape(own_rows, width).astype(jnp.bfloat16)


def solution(mesh):
    placed = (
        P(("groups", "ep", "tp"), None),
        P(),
        P(),
        P(),
        P(("groups", "ep"), None),
        P(("groups", "ep"), None),
        P("ep", "tp", None),
        P("ep", "tp", None),
        P("ep", None, "tp"),
        P("ep", None, None),
    )
    return jax.shard_map(
        body, mesh=mesh, in_specs=placed, out_specs=P(("groups", "ep", "tp"), None), check_vma=False
    )
```

```python
import functools

import jax
import jax.numpy as jnp
from jax import lax
from jax.experimental import pallas as pl
from jax.experimental.pallas import tpu as pltpu
from jax.sharding import PartitionSpec as P

LANES = 128
META = 128
MIB = 1 << 20
RING = 7


def exact_dot(left, right):
    return jnp.dot(
        left, right, precision=lax.Precision.HIGHEST, preferred_element_type=jnp.float32
    )


def prelude_kernel(held_halves, experts, ep_count, tp_count, *refs):
    given, out, held, sems = refs[:6], refs[6], refs[7:13], refs[13]
    copies = [pltpu.make_async_copy(a, b, sems.at[i]) for i, (a, b) in enumerate(zip(given, held))]
    for copy in copies:
        copy.start()
    for copy in copies:
        copy.wait()
    hidden, norm_gain, rot_left, rot_right, ids, weights = held
    own_rows, width = hidden.shape
    factor = rot_left.shape[0]
    tiles = width // LANES
    pack = LANES // factor
    top_count = ids.shape[1]
    values = hidden[...].astype(jnp.float32)
    mean_square = jnp.sum(values * values, axis=1, keepdims=True) / width
    normed = values * lax.rsqrt(mean_square + 1e-06) * norm_gain[...]
    lines = jnp.concatenate(
        [normed[:, t * LANES : (t + 1) * LANES] for t in range(tiles)], axis=0
    )
    right = rot_right[...]
    two = jnp.concatenate([right] * pack, axis=0)
    two = jnp.concatenate([two] * pack, axis=1)
    square = (LANES, LANES)
    line = lax.broadcasted_iota(jnp.int32, square, 0)
    lane = lax.broadcasted_iota(jnp.int32, square, 1)
    two = jnp.where(line // factor == lane // factor, two, 0.0)
    lines = lax.dot_general(
        lines,
        two,
        (((1,), (1,)), ((), ())),
        precision=lax.Precision.HIGHEST,
        preferred_element_type=jnp.float32,
    )
    count = tiles * own_rows
    tall = (count, factor)
    tile_of = lax.broadcasted_iota(jnp.int32, tall, 0) // own_rows
    column = lax.broadcasted_iota(jnp.int32, tall, 1)
    picks = [jnp.where(column == pack * tile_of + p, 1.0, 0.0) for p in range(pack)]
    same_row = (
        lax.broadcasted_iota(jnp.int32, (count, count), 0) % own_rows
        == lax.broadcasted_iota(jnp.int32, (count, count), 1) % own_rows
    )
    chosen = exact_dot(jnp.concatenate(picks, axis=0), rot_left[...])
    turned = jnp.zeros((count, LANES), jnp.float32)
    for p_in in range(pack):
        wide = lax.dot_general(
            chosen,
            picks[p_in],
            (((1,), (1,)), ((), ())),
            precision=lax.Precision.HIGHEST,
            preferred_element_type=jnp.float32,
        )
        for p_out in range(pack):
            block = jnp.where(same_row, wide[p_out * count : (p_out + 1) * count, :], 0.0)
            value = exact_dot(block, lines)
            shift = ((p_out - p_in) * factor) % LANES
            if shift:
                value = pltpu.roll(value, shift, 1)
            turned = turned + jnp.where(
                lax.broadcasted_iota(jnp.int32, (count, LANES), 1) // factor == p_out, value, 0.0
            )
    rotated = jnp.concatenate(
        [turned[t * own_rows : (t + 1) * own_rows, :] for t in range(tiles)], axis=1
    ).astype(jnp.bfloat16)

    gate_weights = weights[...]
    share = (gate_weights / jnp.sum(gate_weights, axis=1, keepdims=True)).astype(jnp.bfloat16)
    both = jnp.concatenate((ids[...].astype(jnp.float32), share.astype(jnp.float32)), axis=1)
    meta = jnp.concatenate(
        [both[t * own_rows : (t + 1) * own_rows, :] for t in range(tp_count)]
        + [jnp.zeros((own_rows, META - 2 * top_count * tp_count), jnp.float32)],
        axis=1,
    )
    spot = lax.broadcasted_iota(jnp.int32, meta.shape, 1) == META - 1
    part_width = width // tp_count
    for e in range(ep_count):
        first = float(e * held_halves % experts)
        tail = jnp.where(spot, first, meta).astype(jnp.bfloat16)
        for t in range(tp_count):
            out[e * tp_count + t, :, :part_width] = rotated[
                :, t * part_width : (t + 1) * part_width
            ]
            out[e * tp_count + t, :, part_width:] = tail


def gate_up_kernel(
    tp_count, top_count, slots, received_ref, w_gate, w_up, part, to_send, spread, inputs, ring, sems
):
    held_halves, part_width, half_ff = w_gate.shape
    depth = ring.shape[0]
    copies = [
        pltpu.make_async_copy(w_up.at[j], ring.at[j % depth], sems.at[j % depth])
        for j in range(held_halves)
    ]
    for j in range(depth):
        copies[j].start()
    peers, own_rows, _ = received_ref.shape
    all_rows = peers * own_rows
    received = received_ref[...].reshape(all_rows, part_width + META)
    meta = received[:, part_width:].astype(jnp.float32).T
    shape = (held_halves, all_rows)
    held = lax.broadcasted_iota(jnp.int32, shape, 0).astype(jnp.float32) + meta[META - 1 :, :]
    group = 2 * top_count
    sender = lax.broadcasted_iota(jnp.int32, (group, all_rows), 1) // own_rows % tp_count
    chosen = meta[:group, :]
    for t in range(1, tp_count):
        chosen = jnp.where(sender == t, meta[t * group : (t + 1) * group, :], chosen)
    member = jnp.zeros(shape, jnp.float32)
    weight = jnp.zeros(shape, jnp.float32)
    for choice in range(top_count):
        named = chosen[choice : choice + 1, :] == held
        member = jnp.where(named, 1.0, member)
        weight = jnp.where(named, chosen[top_count + choice : top_count + choice + 1, :], weight)
    square = (all_rows, all_rows)
    earlier = lax.broadcasted_iota(jnp.int32, square, 0) < lax.broadcasted_iota(
        jnp.int32, square, 1
    )
    rank = jnp.dot(
        member.astype(jnp.bfloat16),
        jnp.where(earlier, 1.0, 0.0).astype(jnp.bfloat16),
        preferred_element_type=jnp.float32,
    )
    rank = jnp.where(member > 0, rank, -1.0)
    slot_index = lax.broadcasted_iota(jnp.int32, (slots, all_rows), 0).astype(jnp.float32)
    selects = []
    for j in range(held_halves):
        select = rank[j : j + 1, :] == slot_index
        selects.append(jnp.where(select, 1.0, 0.0))
        spread[j * slots : (j + 1) * slots, :] = jnp.where(
            select, weight[j : j + 1, :], 0.0
        ).astype(jnp.bfloat16)
    select = jnp.concatenate(selects, axis=0).astype(jnp.bfloat16)
    inputs[...] = jnp.dot(
        select, received[:, :part_width], preferred_element_type=jnp.float32
    ).astype(jnp.bfloat16)
    for index in range(2):
        for j in range(held_halves):
            window = slice(j * slots, (j + 1) * slots)
            if index == 0:
                held_weight = w_gate[j]
            else:
                copies[j].wait()
                held_weight = ring[j % depth]
            value = jnp.dot(inputs[window, :], held_weight, preferred_element_type=jnp.float32)
            part[index, window, :] = value
            to_send[index, window, :] = value.astype(jnp.bfloat16)
            if index == 1 and j + depth < held_halves:
                copies[j + depth].start()


def down_kernel(slots, part, other, unit_scales, spread, w_down, out, lines):
    for j in range(w_down.shape[0]):
        window = slice(j * slots, (j + 1) * slots)
        gate = (part[0, window, :] + other[0, window, :].astype(jnp.float32)) * unit_scales[
            j, 0:1, :
        ]
        up = (part[1, window, :] + other[1, window, :].astype(jnp.float32)) * unit_scales[
            j, 1:2, :
        ]
        units = (gate / (1.0 + jnp.exp(-gate)) * up).astype(jnp.bfloat16)
        lines[window, :] = jnp.dot(
            units, w_down[j], preferred_element_type=jnp.float32
        ).astype(jnp.bfloat16)
    out[...] = lax.dot_general(
        spread[...], lines[...], (((0,), (0,)), ((), ())), preferred_element_type=jnp.float32
    ).astype(jnp.bfloat16)


def body(
    hidden,
    norm_gain,
    rot_left,
    rot_right,
    expert_ids,
    gate_weights,
    w_gate,
    w_up,
    w_down,
    unit_scales,
):
    ep_count = lax.axis_size("ep")
    tp_count = lax.axis_size("tp")
    peers = ep_count * tp_count
    own_rows, width = hidden.shape
    part_width = width // tp_count
    group_rows, top_count = expert_ids.shape
    held_halves, _, half_ff = w_gate.shape
    experts = held_halves * ep_count // 2
    capacity = 5 * group_rows * top_count // (2 * experts)
    slots = capacity * ep_count
    all_rows = peers * own_rows
    lines = held_halves * slots
    depth = min(RING, held_halves)

    vmem = pl.BlockSpec(memory_space=pltpu.VMEM)
    given = (hidden, norm_gain[None, :], rot_left, rot_right, expert_ids, gate_weights)
    outgoing = pl.pallas_call(
        functools.partial(prelude_kernel, held_halves, experts, ep_count, tp_count),
        out_shape=pltpu.VMEM((peers, own_rows, part_width + META), jnp.bfloat16),
        in_specs=[pl.BlockSpec(memory_space=pltpu.HBM)] * len(given),
        out_specs=vmem,
        scratch_shapes=[pltpu.VMEM(array.shape, array.dtype) for array in given]
        + [pltpu.SemaphoreType.DMA((len(given),))],
        cost_estimate=pl.CostEstimate(flops=1 << 36, bytes_accessed=MIB, transcendentals=0),
        compiler_params=pltpu.CompilerParams(vmem_limit_bytes=4 * MIB),
        name="prelude",
    )(*[pltpu.with_memory_space_constraint(array, pltpu.HBM) for array in given])
    received = lax.all_to_all(outgoing, ("ep", "tp"), split_axis=0, concat_axis=0, tiled=True)
    part, to_send, spread = pl.pallas_call(
        functools.partial(gate_up_kernel, tp_count, top_count, slots),
        out_shape=(
            pltpu.VMEM((2, lines, half_ff), jnp.float32),
            pltpu.VMEM((2, lines, half_ff), jnp.bfloat16),
            pltpu.VMEM((lines, all_rows), jnp.bfloat16),
        ),
        in_specs=[vmem, vmem, pl.BlockSpec(memory_space=pltpu.HBM)],
        out_specs=(vmem,) * 3,
        scratch_shapes=[
            pltpu.VMEM((lines, part_width), jnp.bfloat16),
            pltpu.VMEM((depth,) + w_up.shape[1:], w_up.dtype),
            pltpu.SemaphoreType.DMA((depth,)),
        ],
        compiler_params=pltpu.CompilerParams(vmem_limit_bytes=13 * MIB),
        name="gate_up",
    )(
        received,
        pltpu.with_memory_space_constraint(w_gate, pltpu.VMEM),
        pltpu.with_memory_space_constraint(w_up, pltpu.HBM),
    )
    other = lax.ppermute(to_send, "tp", [(i, i ^ 1) for i in range(tp_count)])
    combined = pl.pallas_call(
        functools.partial(down_kernel, slots),
        out_shape=jax.ShapeDtypeStruct((all_rows, part_width), jnp.bfloat16),
        in_specs=[vmem] * 5,
        out_specs=vmem,
        scratch_shapes=[pltpu.VMEM((lines, part_width), jnp.bfloat16)],
        compiler_params=pltpu.CompilerParams(vmem_limit_bytes=5 * MIB),
        name="down",
    )(part, other, unit_scales, spread, pltpu.with_memory_space_constraint(w_down, pltpu.VMEM))
    returned = lax.all_to_all(
        combined.reshape(peers, own_rows, part_width),
        ("ep", "tp"),
        split_axis=0,
        concat_axis=0,
        tiled=True,
    )
    returned = returned.reshape(ep_count, tp_count, own_rows, part_width)
    total = jnp.sum(returned.astype(jnp.float32), axis=0)
    return total.transpose(1, 0, 2).reshape(own_rows, width).astype(jnp.bfloat16)


def solution(mesh):
    placed = (
        P(("groups", "ep", "tp"), None),
        P(),
        P(),
        P(),
        P(("groups", "ep"), None),
        P(("groups", "ep"), None),
        P("ep", "tp", None),
        P("ep", "tp", None),
        P("ep", None, "tp"),
        P("ep", None, None),
    )
    return jax.shard_map(
        body, mesh=mesh, in_specs=placed, out_specs=P(("groups", "ep", "tp"), None), check_vma=False
    )
```

```python
import functools

import jax
import jax.numpy as jnp
from jax import lax
from jax.experimental import pallas as pl
from jax.experimental.pallas import tpu as pltpu
from jax.sharding import PartitionSpec as P

LANES = 128
META = 128
MIB = 1 << 20
RING = 7


def exact_dot(left, right):
    return jnp.dot(
        left, right, precision=lax.Precision.HIGHEST, preferred_element_type=jnp.float32
    )


def prelude_kernel(held_halves, experts, ep_count, tp_count, *refs):
    given, out, held, sems = refs[:6], refs[6], refs[7:13], refs[13]
    copies = [pltpu.make_async_copy(a, b, sems.at[i]) for i, (a, b) in enumerate(zip(given, held))]
    for copy in copies:
        copy.start()
    for copy in copies:
        copy.wait()
    hidden, norm_gain, rot_left, rot_right, ids, weights = held
    own_rows, width = hidden.shape
    factor = rot_left.shape[0]
    tiles = width // LANES
    pack = LANES // factor
    top_count = ids.shape[1]
    values = hidden[...].astype(jnp.float32)
    mean_square = jnp.sum(values * values, axis=1, keepdims=True) / width
    normed = values * lax.rsqrt(mean_square + 1e-06) * norm_gain[...]
    lines = jnp.concatenate(
        [normed[:, t * LANES : (t + 1) * LANES] for t in range(tiles)], axis=0
    )
    right = rot_right[...]
    two = jnp.concatenate([right] * pack, axis=0)
    two = jnp.concatenate([two] * pack, axis=1)
    square = (LANES, LANES)
    line = lax.broadcasted_iota(jnp.int32, square, 0)
    lane = lax.broadcasted_iota(jnp.int32, square, 1)
    two = jnp.where(line // factor == lane // factor, two, 0.0)
    lines = lax.dot_general(
        lines,
        two,
        (((1,), (1,)), ((), ())),
        precision=lax.Precision.HIGHEST,
        preferred_element_type=jnp.float32,
    )
    count = tiles * own_rows
    tall = (count, factor)
    tile_of = lax.broadcasted_iota(jnp.int32, tall, 0) // own_rows
    column = lax.broadcasted_iota(jnp.int32, tall, 1)
    picks = [jnp.where(column == pack * tile_of + p, 1.0, 0.0) for p in range(pack)]
    same_row = (
        lax.broadcasted_iota(jnp.int32, (count, count), 0) % own_rows
        == lax.broadcasted_iota(jnp.int32, (count, count), 1) % own_rows
    )
    chosen = exact_dot(jnp.concatenate(picks, axis=0), rot_left[...])
    turned = jnp.zeros((count, LANES), jnp.float32)
    for p_in in range(pack):
        wide = lax.dot_general(
            chosen,
            picks[p_in],
            (((1,), (1,)), ((), ())),
            precision=lax.Precision.HIGHEST,
            preferred_element_type=jnp.float32,
        )
        for p_out in range(pack):
            block = jnp.where(same_row, wide[p_out * count : (p_out + 1) * count, :], 0.0)
            value = exact_dot(block, lines)
            shift = ((p_out - p_in) * factor) % LANES
            if shift:
                value = pltpu.roll(value, shift, 1)
            turned = turned + jnp.where(
                lax.broadcasted_iota(jnp.int32, (count, LANES), 1) // factor == p_out, value, 0.0
            )
    rotated = jnp.concatenate(
        [turned[t * own_rows : (t + 1) * own_rows, :] for t in range(tiles)], axis=1
    ).astype(jnp.bfloat16)

    gate_weights = weights[...]
    share = (gate_weights / jnp.sum(gate_weights, axis=1, keepdims=True)).astype(jnp.bfloat16)
    both = jnp.concatenate((ids[...].astype(jnp.float32), share.astype(jnp.float32)), axis=1)
    meta = jnp.concatenate(
        [both[t * own_rows : (t + 1) * own_rows, :] for t in range(tp_count)]
        + [jnp.zeros((own_rows, META - 2 * top_count * tp_count), jnp.float32)],
        axis=1,
    )
    spot = lax.broadcasted_iota(jnp.int32, meta.shape, 1) == META - 1
    part_width = width // tp_count
    for e in range(ep_count):
        first = float(e * held_halves % experts)
        tail = jnp.where(spot, first, meta).astype(jnp.bfloat16)
        for t in range(tp_count):
            out[e * tp_count + t, :, :part_width] = rotated[
                :, t * part_width : (t + 1) * part_width
            ]
            out[e * tp_count + t, :, part_width:] = tail


def gate_up_kernel(
    tp_count, top_count, slots, received_ref, w_gate, w_up, part, to_send, spread, inputs, ring, sems
):
    held_halves, part_width, half_ff = w_gate.shape
    depth = ring.shape[0]
    copies = [
        pltpu.make_async_copy(w_up.at[j], ring.at[j % depth], sems.at[j % depth])
        for j in range(held_halves)
    ]
    for j in range(depth):
        copies[j].start()
    peers, own_rows, _ = received_ref.shape
    all_rows = peers * own_rows
    received = received_ref[...].reshape(all_rows, part_width + META)
    meta = received[:, part_width:].astype(jnp.float32).T
    shape = (held_halves, all_rows)
    held = lax.broadcasted_iota(jnp.int32, shape, 0).astype(jnp.float32) + meta[META - 1 :, :]
    group = 2 * top_count
    sender = lax.broadcasted_iota(jnp.int32, (group, all_rows), 1) // own_rows % tp_count
    chosen = meta[:group, :]
    for t in range(1, tp_count):
        chosen = jnp.where(sender == t, meta[t * group : (t + 1) * group, :], chosen)
    member = jnp.zeros(shape, jnp.float32)
    weight = jnp.zeros(shape, jnp.float32)
    for choice in range(top_count):
        named = chosen[choice : choice + 1, :] == held
        member = jnp.where(named, 1.0, member)
        weight = jnp.where(named, chosen[top_count + choice : top_count + choice + 1, :], weight)
    square = (all_rows, all_rows)
    earlier = lax.broadcasted_iota(jnp.int32, square, 0) < lax.broadcasted_iota(
        jnp.int32, square, 1
    )
    rank = jnp.dot(
        member.astype(jnp.bfloat16),
        jnp.where(earlier, 1.0, 0.0).astype(jnp.bfloat16),
        preferred_element_type=jnp.float32,
    )
    rank = jnp.where(member > 0, rank, -1.0)
    slot_index = lax.broadcasted_iota(jnp.int32, (slots, all_rows), 0).astype(jnp.float32)
    selects = []
    for j in range(held_halves):
        select = rank[j : j + 1, :] == slot_index
        selects.append(jnp.where(select, 1.0, 0.0))
        spread[j * slots : (j + 1) * slots, :] = jnp.where(
            select, weight[j : j + 1, :], 0.0
        ).astype(jnp.bfloat16)
    select = jnp.concatenate(selects, axis=0).astype(jnp.bfloat16)
    inputs[...] = jnp.dot(
        select, received[:, :part_width], preferred_element_type=jnp.float32
    ).astype(jnp.bfloat16)
    for j in range(held_halves):
        window = slice(j * slots, (j + 1) * slots)
        for index in range(2):
            if index == 0:
                held_weight = w_gate[j]
            else:
                copies[j].wait()
                held_weight = ring[j % depth]
            value = jnp.dot(inputs[window, :], held_weight, preferred_element_type=jnp.float32)
            part[index, window, :] = value
            to_send[index, window, :] = value.astype(jnp.bfloat16)
        if j + depth < held_halves:
            copies[j + depth].start()


def down_kernel(slots, part, other, unit_scales, spread, w_down, out, lines):
    for j in range(w_down.shape[0]):
        window = slice(j * slots, (j + 1) * slots)
        gate = (part[0, window, :] + other[0, window, :].astype(jnp.float32)) * unit_scales[
            j, 0:1, :
        ]
        up = (part[1, window, :] + other[1, window, :].astype(jnp.float32)) * unit_scales[
            j, 1:2, :
        ]
        units = (gate / (1.0 + jnp.exp(-gate)) * up).astype(jnp.bfloat16)
        lines[window, :] = jnp.dot(
            units, w_down[j], preferred_element_type=jnp.float32
        ).astype(jnp.bfloat16)
    out[...] = lax.dot_general(
        spread[...], lines[...], (((0,), (0,)), ((), ())), preferred_element_type=jnp.float32
    ).astype(jnp.bfloat16)


def body(
    hidden,
    norm_gain,
    rot_left,
    rot_right,
    expert_ids,
    gate_weights,
    w_gate,
    w_up,
    w_down,
    unit_scales,
):
    ep_count = lax.axis_size("ep")
    tp_count = lax.axis_size("tp")
    peers = ep_count * tp_count
    own_rows, width = hidden.shape
    part_width = width // tp_count
    group_rows, top_count = expert_ids.shape
    held_halves, _, half_ff = w_gate.shape
    experts = held_halves * ep_count // 2
    capacity = 5 * group_rows * top_count // (2 * experts)
    slots = capacity * ep_count
    all_rows = peers * own_rows
    lines = held_halves * slots
    depth = min(RING, held_halves)

    vmem = pl.BlockSpec(memory_space=pltpu.VMEM)
    given = (hidden, norm_gain[None, :], rot_left, rot_right, expert_ids, gate_weights)
    outgoing = pl.pallas_call(
        functools.partial(prelude_kernel, held_halves, experts, ep_count, tp_count),
        out_shape=pltpu.VMEM((peers, own_rows, part_width + META), jnp.bfloat16),
        in_specs=[pl.BlockSpec(memory_space=pltpu.HBM)] * len(given),
        out_specs=vmem,
        scratch_shapes=[pltpu.VMEM(array.shape, array.dtype) for array in given]
        + [pltpu.SemaphoreType.DMA((len(given),))],
        cost_estimate=pl.CostEstimate(flops=1 << 36, bytes_accessed=MIB, transcendentals=0),
        compiler_params=pltpu.CompilerParams(vmem_limit_bytes=4 * MIB),
        name="prelude",
    )(*[pltpu.with_memory_space_constraint(array, pltpu.HBM) for array in given])
    received = lax.all_to_all(outgoing, ("ep", "tp"), split_axis=0, concat_axis=0, tiled=True)
    part, to_send, spread = pl.pallas_call(
        functools.partial(gate_up_kernel, tp_count, top_count, slots),
        out_shape=(
            pltpu.VMEM((2, lines, half_ff), jnp.float32),
            pltpu.VMEM((2, lines, half_ff), jnp.bfloat16),
            pltpu.VMEM((lines, all_rows), jnp.bfloat16),
        ),
        in_specs=[vmem, vmem, pl.BlockSpec(memory_space=pltpu.HBM)],
        out_specs=(vmem,) * 3,
        scratch_shapes=[
            pltpu.VMEM((lines, part_width), jnp.bfloat16),
            pltpu.VMEM((depth,) + w_up.shape[1:], w_up.dtype),
            pltpu.SemaphoreType.DMA((depth,)),
        ],
        compiler_params=pltpu.CompilerParams(vmem_limit_bytes=13 * MIB),
        name="gate_up",
    )(
        received,
        pltpu.with_memory_space_constraint(w_gate, pltpu.VMEM),
        pltpu.with_memory_space_constraint(w_up, pltpu.HBM),
    )
    other = lax.ppermute(to_send, "tp", [(i, i ^ 1) for i in range(tp_count)])
    combined = pl.pallas_call(
        functools.partial(down_kernel, slots),
        out_shape=jax.ShapeDtypeStruct((all_rows, part_width), jnp.bfloat16),
        in_specs=[vmem] * 5,
        out_specs=vmem,
        scratch_shapes=[pltpu.VMEM((lines, part_width), jnp.bfloat16)],
        compiler_params=pltpu.CompilerParams(vmem_limit_bytes=5 * MIB),
        name="down",
    )(part, other, unit_scales, spread, pltpu.with_memory_space_constraint(w_down, pltpu.VMEM))
    returned = lax.all_to_all(
        combined.reshape(peers, own_rows, part_width),
        ("ep", "tp"),
        split_axis=0,
        concat_axis=0,
        tiled=True,
    )
    returned = returned.reshape(ep_count, tp_count, own_rows, part_width)
    total = jnp.sum(returned.astype(jnp.float32), axis=0)
    return total.transpose(1, 0, 2).reshape(own_rows, width).astype(jnp.bfloat16)


def solution(mesh):
    placed = (
        P(("groups", "ep", "tp"), None),
        P(),
        P(),
        P(),
        P(("groups", "ep"), None),
        P(("groups", "ep"), None),
        P("ep", "tp", None),
        P("ep", "tp", None),
        P("ep", None, "tp"),
        P("ep", None, None),
    )
    return jax.shard_map(
        body, mesh=mesh, in_specs=placed, out_specs=P(("groups", "ep", "tp"), None), check_vma=False
    )
```

```python
import functools

import jax
import jax.numpy as jnp
from jax import lax
from jax.experimental import pallas as pl
from jax.experimental.pallas import tpu as pltpu
from jax.sharding import PartitionSpec as P

LANES = 128
META = 128
MIB = 1 << 20
DOWN_SHARES = (5, 6, 1)


def exact_dot(left, right):
    return jnp.dot(
        left, right, precision=lax.Precision.HIGHEST, preferred_element_type=jnp.float32
    )


def prelude_kernel(held_halves, experts, ep_count, tp_count, *refs):
    given, out, held, sems = refs[:6], refs[6], refs[7:13], refs[13]
    copies = [pltpu.make_async_copy(a, b, sems.at[i]) for i, (a, b) in enumerate(zip(given, held))]
    for copy in copies:
        copy.start()
    for copy in copies:
        copy.wait()
    hidden, norm_gain, rot_left, rot_right, ids, weights = held
    own_rows, width = hidden.shape
    factor = rot_left.shape[0]
    tiles = width // LANES
    pack = LANES // factor
    top_count = ids.shape[1]
    values = hidden[...].astype(jnp.float32)
    mean_square = jnp.sum(values * values, axis=1, keepdims=True) / width
    normed = values * lax.rsqrt(mean_square + 1e-06) * norm_gain[...]
    lines = jnp.concatenate(
        [normed[:, t * LANES : (t + 1) * LANES] for t in range(tiles)], axis=0
    )
    right = rot_right[...]
    two = jnp.concatenate([right] * pack, axis=0)
    two = jnp.concatenate([two] * pack, axis=1)
    square = (LANES, LANES)
    line = lax.broadcasted_iota(jnp.int32, square, 0)
    lane = lax.broadcasted_iota(jnp.int32, square, 1)
    two = jnp.where(line // factor == lane // factor, two, 0.0)
    lines = lax.dot_general(
        lines,
        two,
        (((1,), (1,)), ((), ())),
        precision=lax.Precision.HIGHEST,
        preferred_element_type=jnp.float32,
    )
    count = tiles * own_rows
    tall = (count, factor)
    tile_of = lax.broadcasted_iota(jnp.int32, tall, 0) // own_rows
    column = lax.broadcasted_iota(jnp.int32, tall, 1)
    picks = [jnp.where(column == pack * tile_of + p, 1.0, 0.0) for p in range(pack)]
    same_row = (
        lax.broadcasted_iota(jnp.int32, (count, count), 0) % own_rows
        == lax.broadcasted_iota(jnp.int32, (count, count), 1) % own_rows
    )
    chosen = exact_dot(jnp.concatenate(picks, axis=0), rot_left[...])
    turned = jnp.zeros((count, LANES), jnp.float32)
    for p_in in range(pack):
        wide = lax.dot_general(
            chosen,
            picks[p_in],
            (((1,), (1,)), ((), ())),
            precision=lax.Precision.HIGHEST,
            preferred_element_type=jnp.float32,
        )
        for p_out in range(pack):
            block = jnp.where(same_row, wide[p_out * count : (p_out + 1) * count, :], 0.0)
            value = exact_dot(block, lines)
            shift = ((p_out - p_in) * factor) % LANES
            if shift:
                value = pltpu.roll(value, shift, 1)
            turned = turned + jnp.where(
                lax.broadcasted_iota(jnp.int32, (count, LANES), 1) // factor == p_out, value, 0.0
            )
    rotated = jnp.concatenate(
        [turned[t * own_rows : (t + 1) * own_rows, :] for t in range(tiles)], axis=1
    ).astype(jnp.bfloat16)

    gate_weights = weights[...]
    share = (gate_weights / jnp.sum(gate_weights, axis=1, keepdims=True)).astype(jnp.bfloat16)
    both = jnp.concatenate((ids[...].astype(jnp.float32), share.astype(jnp.float32)), axis=1)
    meta = jnp.concatenate(
        [both[t * own_rows : (t + 1) * own_rows, :] for t in range(tp_count)]
        + [jnp.zeros((own_rows, META - 2 * top_count * tp_count), jnp.float32)],
        axis=1,
    )
    spot = lax.broadcasted_iota(jnp.int32, meta.shape, 1) == META - 1
    part_width = width // tp_count
    for e in range(ep_count):
        first = float(e * held_halves % experts)
        tail = jnp.where(spot, first, meta).astype(jnp.bfloat16)
        for t in range(tp_count):
            out[e * tp_count + t, :, :part_width] = rotated[
                :, t * part_width : (t + 1) * part_width
            ]
            out[e * tp_count + t, :, part_width:] = tail


def bring(w_down, first, held, sems):
    copies = [
        pltpu.make_async_copy(w_down.at[first + i], held.at[i], sems.at[i])
        for i in range(held.shape[0])
    ]

    def start(i, carry):
        pltpu.make_async_copy(w_down.at[first + i], held.at[i], sems.at[i]).start()
        return carry

    lax.fori_loop(0, len(copies), start, 0)
    return copies


def gate_kernel(tp_count, top_count, slots, received_ref, w_gate, w_down, part, spread, inputs, *more):
    held_halves, part_width, half_ff = w_gate.shape
    copies = bring(w_down, 0, *more) if more else []
    peers, own_rows, _ = received_ref.shape
    all_rows = peers * own_rows
    received = received_ref[...].reshape(all_rows, part_width + META)
    meta = received[:, part_width:].astype(jnp.float32).T
    shape = (held_halves, all_rows)
    held = lax.broadcasted_iota(jnp.int32, shape, 0).astype(jnp.float32) + meta[META - 1 :, :]
    group = 2 * top_count
    sender = lax.broadcasted_iota(jnp.int32, (group, all_rows), 1) // own_rows % tp_count
    chosen = meta[:group, :]
    for t in range(1, tp_count):
        chosen = jnp.where(sender == t, meta[t * group : (t + 1) * group, :], chosen)
    member = jnp.zeros(shape, jnp.float32)
    weight = jnp.zeros(shape, jnp.float32)
    for choice in range(top_count):
        named = chosen[choice : choice + 1, :] == held
        member = jnp.where(named, 1.0, member)
        weight = jnp.where(named, chosen[top_count + choice : top_count + choice + 1, :], weight)
    square = (all_rows, all_rows)
    earlier = lax.broadcasted_iota(jnp.int32, square, 0) < lax.broadcasted_iota(
        jnp.int32, square, 1
    )
    rank = jnp.dot(
        member.astype(jnp.bfloat16),
        jnp.where(earlier, 1.0, 0.0).astype(jnp.bfloat16),
        preferred_element_type=jnp.float32,
    )
    rank = jnp.where(member > 0, rank, -1.0)
    slot_index = lax.broadcasted_iota(jnp.int32, (slots, all_rows), 0).astype(jnp.float32)
    selects = []
    for j in range(held_halves):
        select = rank[j : j + 1, :] == slot_index
        selects.append(jnp.where(select, 1.0, 0.0))
        spread[j * slots : (j + 1) * slots, :] = jnp.where(
            select, weight[j : j + 1, :], 0.0
        ).astype(jnp.bfloat16)
    select = jnp.concatenate(selects, axis=0).astype(jnp.bfloat16)
    inputs[...] = jnp.dot(
        select, received[:, :part_width], preferred_element_type=jnp.float32
    ).astype(jnp.bfloat16)
    for j in range(held_halves):
        window = slice(j * slots, (j + 1) * slots)
        part[window, :] = jnp.dot(
            inputs[window, :], w_gate[j], preferred_element_type=jnp.float32
        )
    for copy in copies:
        copy.wait()


def up_kernel(slots, first, inputs, gate_part, w_up, w_down, part, to_send, *more):
    copies = bring(w_down, first, *more) if more else []
    for j in range(w_up.shape[0]):
        window = slice(j * slots, (j + 1) * slots)
        value = jnp.dot(inputs[window, :], w_up[j], preferred_element_type=jnp.float32)
        part[window, :] = value
        to_send[0, window, :] = gate_part[window, :].astype(jnp.bfloat16)
        to_send[1, window, :] = value.astype(jnp.bfloat16)
    for copy in copies:
        copy.wait()


def bring_kernel(first, after, w_down, *more):
    del after
    for copy in bring(w_down, first, *more):
        copy.wait()


def down_kernel(slots, gate_part, up_part, other, unit_scales, spread, w_down, *more):
    *brought, out, lines, rest, sems = more
    first = sum(held.shape[0] for held in brought)
    copies = bring(w_down, first, rest, sems)
    held = [ref.at[i] for ref in (*brought, rest) for i in range(ref.shape[0])]
    all_units = []
    for j in range(w_down.shape[0]):
        window = slice(j * slots, (j + 1) * slots)
        gate = (gate_part[window, :] + other[0, window, :].astype(jnp.float32)) * unit_scales[
            j, 0:1, :
        ]
        up = (up_part[window, :] + other[1, window, :].astype(jnp.float32)) * unit_scales[
            j, 1:2, :
        ]
        all_units.append((gate / (1.0 + jnp.exp(-gate)) * up).astype(jnp.bfloat16))
    for j in range(w_down.shape[0]):
        if j >= first:
            copies[j - first].wait()
        lines[j * slots : (j + 1) * slots, :] = jnp.dot(
            all_units[j], held[j][...], preferred_element_type=jnp.float32
        ).astype(jnp.bfloat16)
    total = lax.dot_general(
        spread[...], lines[...], (((0,), (0,)), ((), ())), preferred_element_type=jnp.float32
    ).astype(jnp.bfloat16)
    out[...] = total.reshape(out.shape)


def body(
    hidden,
    norm_gain,
    rot_left,
    rot_right,
    expert_ids,
    gate_weights,
    w_gate,
    w_up,
    w_down,
    unit_scales,
):
    ep_count = lax.axis_size("ep")
    tp_count = lax.axis_size("tp")
    peers = ep_count * tp_count
    own_rows, width = hidden.shape
    part_width = width // tp_count
    group_rows, top_count = expert_ids.shape
    held_halves, _, half_ff = w_gate.shape
    experts = held_halves * ep_count // 2
    capacity = 5 * group_rows * top_count // (2 * experts)
    slots = capacity * ep_count
    all_rows = peers * own_rows
    lines = held_halves * slots

    vmem = pl.BlockSpec(memory_space=pltpu.VMEM)
    given = (hidden, norm_gain[None, :], rot_left, rot_right, expert_ids, gate_weights)
    outgoing = pl.pallas_call(
        functools.partial(prelude_kernel, held_halves, experts, ep_count, tp_count),
        out_shape=pltpu.VMEM((peers, own_rows, part_width + META), jnp.bfloat16),
        in_specs=[pl.BlockSpec(memory_space=pltpu.HBM)] * len(given),
        out_specs=vmem,
        scratch_shapes=[pltpu.VMEM(array.shape, array.dtype) for array in given]
        + [pltpu.SemaphoreType.DMA((len(given),))],
        cost_estimate=pl.CostEstimate(flops=1 << 36, bytes_accessed=MIB, transcendentals=0),
        compiler_params=pltpu.CompilerParams(vmem_limit_bytes=2 * MIB),
        name="prelude",
    )(*[pltpu.with_memory_space_constraint(array, pltpu.HBM) for array in given])
    received = lax.all_to_all(outgoing, ("ep", "tp"), split_axis=0, concat_axis=0, tiled=True)
    in_vmem, in_hbm = (
        functools.partial(pltpu.with_memory_space_constraint, memory_space=space)
        for space in (pltpu.VMEM, pltpu.HBM)
    )
    hbm = pl.BlockSpec(memory_space=pltpu.HBM)

    def brought(count):
        shapes = [pltpu.VMEM((count,) + w_down.shape[1:], w_down.dtype)] if count else []
        return shapes, [pltpu.SemaphoreType.DMA((count,))] if count else []

    counts = [held_halves * share // 16 for share in DOWN_SHARES]
    shapes, sems = brought(counts[0])
    gate_part, spread, inputs, *first_down = pl.pallas_call(
        functools.partial(gate_kernel, tp_count, top_count, slots),
        out_shape=[
            pltpu.VMEM((lines, half_ff), jnp.float32),
            pltpu.VMEM((lines, all_rows), jnp.bfloat16),
            pltpu.VMEM((lines, part_width), jnp.bfloat16),
        ]
        + shapes,
        in_specs=[vmem, vmem, hbm],
        out_specs=[vmem] * (3 + len(shapes)),
        scratch_shapes=sems,
        compiler_params=pltpu.CompilerParams(vmem_limit_bytes=2 * MIB),
        name="gate",
    )(received, in_vmem(w_gate), in_hbm(w_down))
    shapes, sems = brought(counts[1])
    up_part, to_send, *next_down = pl.pallas_call(
        functools.partial(up_kernel, slots, counts[0]),
        out_shape=[
            pltpu.VMEM((lines, half_ff), jnp.float32),
            pltpu.VMEM((2, lines, half_ff), jnp.bfloat16),
        ]
        + shapes,
        in_specs=[vmem, vmem, vmem, hbm],
        out_specs=[vmem] * (2 + len(shapes)),
        scratch_shapes=sems,
        compiler_params=pltpu.CompilerParams(vmem_limit_bytes=2 * MIB),
        name="up",
    )(in_vmem(inputs), in_vmem(gate_part), in_vmem(w_up), in_hbm(w_down))
    other = lax.ppermute(to_send, "tp", [(i, i ^ 1) for i in range(tp_count)])
    shapes, sems = brought(counts[2])
    last_down = []
    if shapes:
        last_down = pl.pallas_call(
            functools.partial(bring_kernel, counts[0] + counts[1]),
            out_shape=shapes,
            in_specs=[vmem, hbm],
            out_specs=[vmem],
            scratch_shapes=sems,
            compiler_params=pltpu.CompilerParams(vmem_limit_bytes=MIB),
            name="bring",
        )(in_vmem(up_part), in_hbm(w_down))
    brought_down = [in_vmem(array) for array in (*first_down, *next_down, *last_down)]
    rest = held_halves - sum(counts)
    combined = pl.pallas_call(
        functools.partial(down_kernel, slots),
        out_shape=jax.ShapeDtypeStruct((peers, own_rows, part_width), jnp.bfloat16),
        in_specs=[vmem] * 5 + [hbm] + [vmem] * len(brought_down),
        out_specs=vmem,
        scratch_shapes=[
            pltpu.VMEM((lines, part_width), jnp.bfloat16),
            pltpu.VMEM((rest,) + w_down.shape[1:], w_down.dtype),
            pltpu.SemaphoreType.DMA((rest,)),
        ],
        compiler_params=pltpu.CompilerParams(vmem_limit_bytes=(2 + 3 * (rest + 1) // 2) * MIB),
        name="down",
    )(
        in_vmem(gate_part),
        in_vmem(up_part),
        other,
        unit_scales,
        in_vmem(spread),
        in_hbm(w_down),
        *brought_down,
    )
    returned = lax.all_to_all(
        combined,
        ("ep", "tp"),
        split_axis=0,
        concat_axis=0,
        tiled=True,
    )
    returned = returned.reshape(ep_count, tp_count, own_rows, part_width)
    total = jnp.sum(returned.astype(jnp.float32), axis=0)
    return total.transpose(1, 0, 2).reshape(own_rows, width).astype(jnp.bfloat16)


def solution(mesh):
    placed = (
        P(("groups", "ep", "tp"), None),
        P(),
        P(),
        P(),
        P(("groups", "ep"), None),
        P(("groups", "ep"), None),
        P("ep", "tp", None),
        P("ep", "tp", None),
        P("ep", None, "tp"),
        P("ep", None, None),
    )
    return jax.shard_map(
        body, mesh=mesh, in_specs=placed, out_specs=P(("groups", "ep", "tp"), None), check_vma=False
    )
```

```python
import functools

import jax
import jax.numpy as jnp
from jax import lax
from jax.experimental import pallas as pl
from jax.experimental.pallas import tpu as pltpu
from jax.sharding import PartitionSpec as P

LANES = 128
META = 128
MIB = 1 << 20
DOWN_SHARES = (5, 6, 1)


def terms(value):
    high = value.astype(jnp.bfloat16)
    return high, (value - high.astype(jnp.float32)).astype(jnp.bfloat16)


def dot(left, right, contract=0):
    return lax.dot_general(
        left, right, (((1,), (contract,)), ((), ())), preferred_element_type=jnp.float32
    )


def prelude_kernel(held_halves, experts, ep_count, tp_count, *refs):
    given, out, held, sems = refs[:6], refs[6], refs[7:13], refs[13]
    copies = [pltpu.make_async_copy(a, b, sems.at[i]) for i, (a, b) in enumerate(zip(given, held))]
    for copy in copies:
        copy.start()
    for copy in copies:
        copy.wait()
    hidden, norm_gain, rot_left, rot_right, ids, weights = held
    own_rows, width = hidden.shape
    factor = rot_left.shape[0]
    tiles = width // LANES
    pack = LANES // factor
    top_count = ids.shape[1]
    values = hidden[...].astype(jnp.float32)
    mean_square = jnp.sum(values * values, axis=1, keepdims=True) / width
    normed = values * lax.rsqrt(mean_square + 1e-06) * norm_gain[...]
    lines = jnp.concatenate(
        [normed[:, t * LANES : (t + 1) * LANES] for t in range(tiles)], axis=0
    )
    two = jnp.concatenate([rot_right[...]] * pack, axis=0)
    two = jnp.concatenate([two] * pack, axis=1)
    square = (LANES, LANES)
    line = lax.broadcasted_iota(jnp.int32, square, 0)
    lane = lax.broadcasted_iota(jnp.int32, square, 1)
    two_high, two_low = terms(jnp.where(line // factor == lane // factor, two, 0.0))
    count = tiles * own_rows
    tall = (count, factor)
    tile_of = lax.broadcasted_iota(jnp.int32, tall, 0) // own_rows
    column = lax.broadcasted_iota(jnp.int32, tall, 1)
    picks = [
        jnp.where(column == pack * tile_of + p, 1.0, 0.0).astype(jnp.bfloat16)
        for p in range(pack)
    ]
    same_row = (
        lax.broadcasted_iota(jnp.int32, (pack * count, count), 0) % own_rows
        == lax.broadcasted_iota(jnp.int32, (pack * count, count), 1) % own_rows
    )
    rows_of = jnp.concatenate(picks, axis=0)
    chosen = [dot(rows_of, term).astype(jnp.bfloat16) for term in terms(rot_left[...])]
    blocks = [
        [jnp.where(same_row, dot(term, picks[p], 1), 0.0).astype(jnp.bfloat16) for term in chosen]
        for p in range(pack)
    ]
    high, low = terms(lines)
    lines = dot(high, two_high, 1) + (dot(high, two_low, 1) + dot(low, two_high, 1))
    high, low = terms(lines)
    turned = jnp.zeros((count, LANES), jnp.float32)
    for p_in in range(pack):
        block_high, block_low = blocks[p_in]
        values = dot(block_high, high) + (dot(block_high, low) + dot(block_low, high))
        for p_out in range(pack):
            value = values[p_out * count : (p_out + 1) * count, :]
            shift = ((p_out - p_in) * factor) % LANES
            if shift:
                value = pltpu.roll(value, shift, 1)
            turned = turned + jnp.where(
                lax.broadcasted_iota(jnp.int32, (count, LANES), 1) // factor == p_out, value, 0.0
            )
    rotated = jnp.concatenate(
        [turned[t * own_rows : (t + 1) * own_rows, :] for t in range(tiles)], axis=1
    ).astype(jnp.bfloat16)

    gate_weights = weights[...]
    share = (gate_weights / jnp.sum(gate_weights, axis=1, keepdims=True)).astype(jnp.bfloat16)
    both = jnp.concatenate((ids[...].astype(jnp.float32), share.astype(jnp.float32)), axis=1)
    meta = jnp.concatenate(
        [both[t * own_rows : (t + 1) * own_rows, :] for t in range(tp_count)]
        + [jnp.zeros((own_rows, META - 2 * top_count * tp_count), jnp.float32)],
        axis=1,
    )
    spot = lax.broadcasted_iota(jnp.int32, meta.shape, 1) == META - 1
    part_width = width // tp_count
    for e in range(ep_count):
        first = float(e * held_halves % experts)
        tail = jnp.where(spot, first, meta).astype(jnp.bfloat16)
        for t in range(tp_count):
            out[e * tp_count + t, :, :part_width] = rotated[
                :, t * part_width : (t + 1) * part_width
            ]
            out[e * tp_count + t, :, part_width:] = tail


def bring(w_down, first, held, sems):
    copies = [
        pltpu.make_async_copy(w_down.at[first + i], held.at[i], sems.at[i])
        for i in range(held.shape[0])
    ]

    def start(i, carry):
        pltpu.make_async_copy(w_down.at[first + i], held.at[i], sems.at[i]).start()
        return carry

    lax.fori_loop(0, len(copies), start, 0)
    return copies


def gate_kernel(tp_count, top_count, slots, received_ref, w_gate, w_down, part, spread, inputs, *more):
    held_halves, part_width, half_ff = w_gate.shape
    copies = bring(w_down, 0, *more) if more else []
    peers, own_rows, _ = received_ref.shape
    all_rows = peers * own_rows
    received = received_ref[...].reshape(all_rows, part_width + META)
    meta = received[:, part_width:].astype(jnp.float32).T
    shape = (held_halves, all_rows)
    held = lax.broadcasted_iota(jnp.int32, shape, 0).astype(jnp.float32) + meta[META - 1 :, :]
    group = 2 * top_count
    sender = lax.broadcasted_iota(jnp.int32, (group, all_rows), 1) // own_rows % tp_count
    chosen = meta[:group, :]
    for t in range(1, tp_count):
        chosen = jnp.where(sender == t, meta[t * group : (t + 1) * group, :], chosen)
    member = jnp.zeros(shape, jnp.float32)
    weight = jnp.zeros(shape, jnp.float32)
    for choice in range(top_count):
        named = chosen[choice : choice + 1, :] == held
        member = jnp.where(named, 1.0, member)
        weight = jnp.where(named, chosen[top_count + choice : top_count + choice + 1, :], weight)
    square = (all_rows, all_rows)
    earlier = lax.broadcasted_iota(jnp.int32, square, 0) < lax.broadcasted_iota(
        jnp.int32, square, 1
    )
    rank = jnp.dot(
        member.astype(jnp.bfloat16),
        jnp.where(earlier, 1.0, 0.0).astype(jnp.bfloat16),
        preferred_element_type=jnp.float32,
    )
    rank = jnp.where(member > 0, rank, -1.0)
    slot_index = lax.broadcasted_iota(jnp.int32, (slots, all_rows), 0).astype(jnp.float32)
    selects = []
    for j in range(held_halves):
        select = rank[j : j + 1, :] == slot_index
        selects.append(jnp.where(select, 1.0, 0.0))
        spread[j * slots : (j + 1) * slots, :] = jnp.where(
            select, weight[j : j + 1, :], 0.0
        ).astype(jnp.bfloat16)
    select = jnp.concatenate(selects, axis=0).astype(jnp.bfloat16)
    inputs[...] = jnp.dot(
        select, received[:, :part_width], preferred_element_type=jnp.float32
    ).astype(jnp.bfloat16)
    for j in range(held_halves):
        window = slice(j * slots, (j + 1) * slots)
        part[window, :] = jnp.dot(
            inputs[window, :], w_gate[j], preferred_element_type=jnp.float32
        )
    for copy in copies:
        copy.wait()


def up_kernel(slots, first, inputs, gate_part, w_up, w_down, part, to_send, *more):
    copies = bring(w_down, first, *more) if more else []
    for j in range(w_up.shape[0]):
        window = slice(j * slots, (j + 1) * slots)
        value = jnp.dot(inputs[window, :], w_up[j], preferred_element_type=jnp.float32)
        part[window, :] = value
        to_send[0, window, :] = gate_part[window, :].astype(jnp.bfloat16)
        to_send[1, window, :] = value.astype(jnp.bfloat16)
    for copy in copies:
        copy.wait()


def bring_kernel(first, after, w_down, *more):
    del after
    for copy in bring(w_down, first, *more):
        copy.wait()


def down_kernel(slots, gate_part, up_part, other, unit_scales, spread, w_down, *more):
    *brought, out, lines, rest, sems = more
    first = sum(held.shape[0] for held in brought)
    copies = bring(w_down, first, rest, sems)
    held = [ref.at[i] for ref in (*brought, rest) for i in range(ref.shape[0])]
    all_units = []
    for j in range(w_down.shape[0]):
        window = slice(j * slots, (j + 1) * slots)
        gate = (gate_part[window, :] + other[0, window, :].astype(jnp.float32)) * unit_scales[
            j, 0:1, :
        ]
        up = (up_part[window, :] + other[1, window, :].astype(jnp.float32)) * unit_scales[
            j, 1:2, :
        ]
        all_units.append((gate / (1.0 + jnp.exp(-gate)) * up).astype(jnp.bfloat16))
    for j in range(w_down.shape[0]):
        if j == first:
            for copy in copies:
                copy.wait()
        lines[j * slots : (j + 1) * slots, :] = jnp.dot(
            all_units[j], held[j][...], preferred_element_type=jnp.float32
        ).astype(jnp.bfloat16)
    total = lax.dot_general(
        spread[...], lines[...], (((0,), (0,)), ((), ())), preferred_element_type=jnp.float32
    ).astype(jnp.bfloat16)
    out[...] = total.reshape(out.shape)


def finish_kernel(ep_count, returned, out):
    tp_count = returned.shape[0] // ep_count
    part_width = returned.shape[2]
    for t in range(tp_count):
        total = returned[t].astype(jnp.float32)
        for e in range(1, ep_count):
            total = total + returned[e * tp_count + t].astype(jnp.float32)
        out[:, t * part_width : (t + 1) * part_width] = total.astype(jnp.bfloat16)


def body(
    hidden,
    norm_gain,
    rot_left,
    rot_right,
    expert_ids,
    gate_weights,
    w_gate,
    w_up,
    w_down,
    unit_scales,
):
    ep_count = lax.axis_size("ep")
    tp_count = lax.axis_size("tp")
    peers = ep_count * tp_count
    own_rows, width = hidden.shape
    part_width = width // tp_count
    group_rows, top_count = expert_ids.shape
    held_halves, _, half_ff = w_gate.shape
    experts = held_halves * ep_count // 2
    capacity = 5 * group_rows * top_count // (2 * experts)
    slots = capacity * ep_count
    all_rows = peers * own_rows
    lines = held_halves * slots

    vmem = pl.BlockSpec(memory_space=pltpu.VMEM)
    given = (hidden, norm_gain[None, :], rot_left, rot_right, expert_ids, gate_weights)
    outgoing = pl.pallas_call(
        functools.partial(prelude_kernel, held_halves, experts, ep_count, tp_count),
        out_shape=pltpu.VMEM((peers, own_rows, part_width + META), jnp.bfloat16),
        in_specs=[pl.BlockSpec(memory_space=pltpu.HBM)] * len(given),
        out_specs=vmem,
        scratch_shapes=[pltpu.VMEM(array.shape, array.dtype) for array in given]
        + [pltpu.SemaphoreType.DMA((len(given),))],
        cost_estimate=pl.CostEstimate(flops=1 << 36, bytes_accessed=MIB, transcendentals=0),
        compiler_params=pltpu.CompilerParams(vmem_limit_bytes=2 * MIB),
        name="prelude",
    )(*[pltpu.with_memory_space_constraint(array, pltpu.HBM) for array in given])
    received = lax.all_to_all(outgoing, ("ep", "tp"), split_axis=0, concat_axis=0, tiled=True)
    in_vmem, in_hbm = (
        functools.partial(pltpu.with_memory_space_constraint, memory_space=space)
        for space in (pltpu.VMEM, pltpu.HBM)
    )
    hbm = pl.BlockSpec(memory_space=pltpu.HBM)

    def brought(count):
        shapes = [pltpu.VMEM((count,) + w_down.shape[1:], w_down.dtype)] if count else []
        return shapes, [pltpu.SemaphoreType.DMA((count,))] if count else []

    counts = [held_halves * share // 16 for share in DOWN_SHARES]
    shapes, sems = brought(counts[0])
    gate_part, spread, inputs, *first_down = pl.pallas_call(
        functools.partial(gate_kernel, tp_count, top_count, slots),
        out_shape=[
            pltpu.VMEM((lines, half_ff), jnp.float32),
            pltpu.VMEM((lines, all_rows), jnp.bfloat16),
            pltpu.VMEM((lines, part_width), jnp.bfloat16),
        ]
        + shapes,
        in_specs=[vmem, vmem, hbm],
        out_specs=[vmem] * (3 + len(shapes)),
        scratch_shapes=sems,
        compiler_params=pltpu.CompilerParams(vmem_limit_bytes=2 * MIB),
        name="gate",
    )(received, in_vmem(w_gate), in_hbm(w_down))
    shapes, sems = brought(counts[1])
    up_part, to_send, *next_down = pl.pallas_call(
        functools.partial(up_kernel, slots, counts[0]),
        out_shape=[
            pltpu.VMEM((lines, half_ff), jnp.float32),
            pltpu.VMEM((2, lines, half_ff), jnp.bfloat16),
        ]
        + shapes,
        in_specs=[vmem, vmem, vmem, hbm],
        out_specs=[vmem] * (2 + len(shapes)),
        scratch_shapes=sems,
        compiler_params=pltpu.CompilerParams(vmem_limit_bytes=2 * MIB),
        name="up",
    )(in_vmem(inputs), in_vmem(gate_part), in_vmem(w_up), in_hbm(w_down))
    other = lax.ppermute(to_send, "tp", [(i, i ^ 1) for i in range(tp_count)])
    shapes, sems = brought(counts[2])
    last_down = []
    if shapes:
        last_down = pl.pallas_call(
            functools.partial(bring_kernel, counts[0] + counts[1]),
            out_shape=shapes,
            in_specs=[vmem, hbm],
            out_specs=[vmem],
            scratch_shapes=sems,
            compiler_params=pltpu.CompilerParams(vmem_limit_bytes=MIB),
            name="bring",
        )(in_vmem(up_part), in_hbm(w_down))
    brought_down = [in_vmem(array) for array in (*first_down, *next_down, *last_down)]
    rest = held_halves - sum(counts)
    combined = pl.pallas_call(
        functools.partial(down_kernel, slots),
        out_shape=jax.ShapeDtypeStruct((peers, own_rows, part_width), jnp.bfloat16),
        in_specs=[vmem] * 5 + [hbm] + [vmem] * len(brought_down),
        out_specs=vmem,
        scratch_shapes=[
            pltpu.VMEM((lines, part_width), jnp.bfloat16),
            pltpu.VMEM((rest,) + w_down.shape[1:], w_down.dtype),
            pltpu.SemaphoreType.DMA((rest,)),
        ],
        compiler_params=pltpu.CompilerParams(vmem_limit_bytes=(2 + 3 * (rest + 1) // 2) * MIB),
        name="down",
    )(
        in_vmem(gate_part),
        in_vmem(up_part),
        other,
        unit_scales,
        in_vmem(spread),
        in_hbm(w_down),
        *brought_down,
    )
    returned = lax.all_to_all(
        combined,
        ("ep", "tp"),
        split_axis=0,
        concat_axis=0,
        tiled=True,
    )
    return pl.pallas_call(
        functools.partial(finish_kernel, ep_count),
        out_shape=jax.ShapeDtypeStruct((own_rows, width), jnp.bfloat16),
        in_specs=[vmem],
        out_specs=vmem,
        compiler_params=pltpu.CompilerParams(vmem_limit_bytes=16 * MIB),
        name="finish",
    )(returned)


def solution(mesh):
    placed = (
        P(("groups", "ep", "tp"), None),
        P(),
        P(),
        P(),
        P(("groups", "ep"), None),
        P(("groups", "ep"), None),
        P("ep", "tp", None),
        P("ep", "tp", None),
        P("ep", None, "tp"),
        P("ep", None, None),
    )
    return jax.shard_map(
        body, mesh=mesh, in_specs=placed, out_specs=P(("groups", "ep", "tp"), None), check_vma=False
    )
```

```python
import functools

import jax
import jax.numpy as jnp
from jax import lax
from jax.experimental import pallas as pl
from jax.experimental.pallas import tpu as pltpu
from jax.sharding import PartitionSpec as P

LANES = 128
META = 128
MIB = 1 << 20
DOWN_SHARES = (5, 6, 1)


def terms(value):
    high = value.astype(jnp.bfloat16)
    return high, (value - high.astype(jnp.float32)).astype(jnp.bfloat16)


def dot(left, right, contract=0):
    return lax.dot_general(
        left, right, (((1,), (contract,)), ((), ())), preferred_element_type=jnp.float32
    )


def prelude_kernel(held_halves, experts, ep_count, tp_count, *refs):
    given, out, held, sems = refs[:6], refs[6], refs[7:13], refs[13]
    copies = [pltpu.make_async_copy(a, b, sems.at[i]) for i, (a, b) in enumerate(zip(given, held))]
    for copy in copies:
        copy.start()
    for copy in copies:
        copy.wait()
    hidden, norm_gain, rot_left, rot_right, ids, weights = held
    own_rows, width = hidden.shape
    factor = rot_left.shape[0]
    tiles = width // LANES
    pack = LANES // factor
    top_count = ids.shape[1]
    values = hidden[...].astype(jnp.float32)
    mean_square = jnp.sum(values * values, axis=1, keepdims=True) / width
    normed = values * lax.rsqrt(mean_square + 1e-06) * norm_gain[...]
    lines = jnp.concatenate(
        [normed[:, t * LANES : (t + 1) * LANES] for t in range(tiles)], axis=0
    )
    two = jnp.concatenate([rot_right[...]] * pack, axis=0)
    two = jnp.concatenate([two] * pack, axis=1)
    square = (LANES, LANES)
    line = lax.broadcasted_iota(jnp.int32, square, 0)
    lane = lax.broadcasted_iota(jnp.int32, square, 1)
    two_high, two_low = terms(jnp.where(line // factor == lane // factor, two, 0.0))
    count = tiles * own_rows
    tall = (count, factor)
    tile_of = lax.broadcasted_iota(jnp.int32, tall, 0) // own_rows
    column = lax.broadcasted_iota(jnp.int32, tall, 1)
    picks = [
        jnp.where(column == pack * tile_of + p, 1.0, 0.0).astype(jnp.bfloat16)
        for p in range(pack)
    ]
    same_row = (
        lax.broadcasted_iota(jnp.int32, (pack * count, count), 0) % own_rows
        == lax.broadcasted_iota(jnp.int32, (pack * count, count), 1) % own_rows
    )
    rows_of = jnp.concatenate(picks, axis=0)
    chosen = [dot(rows_of, term).astype(jnp.bfloat16) for term in terms(rot_left[...])]
    blocks = [
        [jnp.where(same_row, dot(term, picks[p], 1), 0.0).astype(jnp.bfloat16) for term in chosen]
        for p in range(pack)
    ]
    high, low = terms(lines)
    lines = dot(high, two_high, 1) + (dot(high, two_low, 1) + dot(low, two_high, 1))
    high, low = terms(lines)
    turned = jnp.zeros((count, LANES), jnp.float32)
    for p_in in range(pack):
        block_high, block_low = blocks[p_in]
        values = dot(block_high, high) + (dot(block_high, low) + dot(block_low, high))
        for p_out in range(pack):
            value = values[p_out * count : (p_out + 1) * count, :]
            shift = ((p_out - p_in) * factor) % LANES
            if shift:
                value = pltpu.roll(value, shift, 1)
            turned = turned + jnp.where(
                lax.broadcasted_iota(jnp.int32, (count, LANES), 1) // factor == p_out, value, 0.0
            )
    rotated = jnp.concatenate(
        [turned[t * own_rows : (t + 1) * own_rows, :] for t in range(tiles)], axis=1
    ).astype(jnp.bfloat16)

    gate_weights = weights[...]
    share = (gate_weights / jnp.sum(gate_weights, axis=1, keepdims=True)).astype(jnp.bfloat16)
    both = jnp.concatenate((ids[...].astype(jnp.float32), share.astype(jnp.float32)), axis=1)
    meta = jnp.concatenate(
        [both[t * own_rows : (t + 1) * own_rows, :] for t in range(tp_count)]
        + [jnp.zeros((own_rows, META - 2 * top_count * tp_count), jnp.float32)],
        axis=1,
    )
    spot = lax.broadcasted_iota(jnp.int32, meta.shape, 1) == META - 1
    part_width = width // tp_count
    for e in range(ep_count):
        first = float(e * held_halves % experts)
        tail = jnp.where(spot, first, meta).astype(jnp.bfloat16)
        for t in range(tp_count):
            out[e * tp_count + t, :, :part_width] = rotated[
                :, t * part_width : (t + 1) * part_width
            ]
            out[e * tp_count + t, :, part_width:] = tail


def bring(w_down, first, held, sems):
    copies = [
        pltpu.make_async_copy(w_down.at[first + i], held.at[i], sems.at[i])
        for i in range(held.shape[0])
    ]

    def start(i, carry):
        pltpu.make_async_copy(w_down.at[first + i], held.at[i], sems.at[i]).start()
        return carry

    lax.fori_loop(0, len(copies), start, 0)
    return copies


def pass_kernel(given, out):
    del given, out


def gate_kernel(tp_count, top_count, slots, received_ref, w_gate, w_down, part, spread, inputs, *more):
    held_halves, part_width, half_ff = w_gate.shape
    copies = bring(w_down, 0, *more) if more else []
    peers, own_rows, _ = received_ref.shape
    all_rows = peers * own_rows
    received = received_ref[...].reshape(all_rows, part_width + META)
    meta = received[:, part_width:].astype(jnp.float32).T
    shape = (held_halves, all_rows)
    held = lax.broadcasted_iota(jnp.int32, shape, 0).astype(jnp.float32) + meta[META - 1 :, :]
    group = 2 * top_count
    sender = lax.broadcasted_iota(jnp.int32, (group, all_rows), 1) // own_rows % tp_count
    chosen = meta[:group, :]
    for t in range(1, tp_count):
        chosen = jnp.where(sender == t, meta[t * group : (t + 1) * group, :], chosen)
    member = jnp.zeros(shape, jnp.float32)
    weight = jnp.zeros(shape, jnp.float32)
    for choice in range(top_count):
        named = chosen[choice : choice + 1, :] == held
        member = jnp.where(named, 1.0, member)
        weight = jnp.where(named, chosen[top_count + choice : top_count + choice + 1, :], weight)
    square = (all_rows, all_rows)
    earlier = lax.broadcasted_iota(jnp.int32, square, 0) < lax.broadcasted_iota(
        jnp.int32, square, 1
    )
    rank = jnp.dot(
        member.astype(jnp.bfloat16),
        jnp.where(earlier, 1.0, 0.0).astype(jnp.bfloat16),
        preferred_element_type=jnp.float32,
    )
    rank = jnp.where(member > 0, rank, -1.0)
    slot_index = lax.broadcasted_iota(jnp.int32, (slots, all_rows), 0).astype(jnp.float32)
    selects = []
    for j in range(held_halves):
        selects.append(jnp.where(rank[j : j + 1, :] == slot_index, 1.0, 0.0))
    select = jnp.concatenate(selects, axis=0).astype(jnp.bfloat16)
    inputs[...] = jnp.dot(
        select, received[:, :part_width], preferred_element_type=jnp.float32
    ).astype(jnp.bfloat16)
    for j in range(held_halves):
        window = slice(j * slots, (j + 1) * slots)
        part[window, :] = jnp.dot(
            inputs[window, :], w_gate[j], preferred_element_type=jnp.float32
        )
    for j in range(held_halves):
        spread[j * slots : (j + 1) * slots, :] = jnp.where(
            rank[j : j + 1, :] == slot_index, weight[j : j + 1, :], 0.0
        ).astype(jnp.bfloat16)
    for copy in copies:
        copy.wait()


def up_kernel(slots, first, inputs, gate_part, w_up, w_down, part, to_send, *more):
    copies = bring(w_down, first, *more) if more else []
    for j in range(w_up.shape[0]):
        window = slice(j * slots, (j + 1) * slots)
        value = jnp.dot(inputs[window, :], w_up[j], preferred_element_type=jnp.float32)
        part[window, :] = value
        to_send[0, window, :] = gate_part[window, :].astype(jnp.bfloat16)
        to_send[1, window, :] = value.astype(jnp.bfloat16)
    for copy in copies:
        copy.wait()


def bring_kernel(first, after, w_down, *more):
    del after
    for copy in bring(w_down, first, *more):
        copy.wait()


def down_kernel(slots, gate_part, up_part, other, unit_scales, spread, w_down, *more):
    *brought, out, lines, rest, sems = more
    first = sum(held.shape[0] for held in brought)
    copies = bring(w_down, first, rest, sems)
    held = [ref.at[i] for ref in (*brought, rest) for i in range(ref.shape[0])]
    all_units = []
    for j in range(w_down.shape[0]):
        window = slice(j * slots, (j + 1) * slots)
        gate = (gate_part[window, :] + other[0, window, :].astype(jnp.float32)) * unit_scales[
            j, 0:1, :
        ]
        up = (up_part[window, :] + other[1, window, :].astype(jnp.float32)) * unit_scales[
            j, 1:2, :
        ]
        all_units.append((gate / (1.0 + jnp.exp(-gate)) * up).astype(jnp.bfloat16))
    for j in range(w_down.shape[0]):
        if j == first:
            for copy in copies:
                copy.wait()
        lines[j * slots : (j + 1) * slots, :] = jnp.dot(
            all_units[j], held[j][...], preferred_element_type=jnp.float32
        ).astype(jnp.bfloat16)
    total = lax.dot_general(
        spread[...], lines[...], (((0,), (0,)), ((), ())), preferred_element_type=jnp.float32
    ).astype(jnp.bfloat16)
    out[...] = total.reshape(out.shape)


def finish_kernel(ep_count, returned, out):
    tp_count = returned.shape[0] // ep_count
    part_width = returned.shape[2]
    for t in range(tp_count):
        total = returned[t].astype(jnp.float32)
        for e in range(1, ep_count):
            total = total + returned[e * tp_count + t].astype(jnp.float32)
        out[:, t * part_width : (t + 1) * part_width] = total.astype(jnp.bfloat16)


def body(
    hidden,
    norm_gain,
    rot_left,
    rot_right,
    expert_ids,
    gate_weights,
    w_gate,
    w_up,
    w_down,
    unit_scales,
):
    ep_count = lax.axis_size("ep")
    tp_count = lax.axis_size("tp")
    peers = ep_count * tp_count
    own_rows, width = hidden.shape
    part_width = width // tp_count
    group_rows, top_count = expert_ids.shape
    held_halves, _, half_ff = w_gate.shape
    experts = held_halves * ep_count // 2
    capacity = 5 * group_rows * top_count // (2 * experts)
    slots = capacity * ep_count
    all_rows = peers * own_rows
    lines = held_halves * slots

    vmem = pl.BlockSpec(memory_space=pltpu.VMEM)
    given = (hidden, norm_gain[None, :], rot_left, rot_right, expert_ids, gate_weights)
    outgoing = pl.pallas_call(
        functools.partial(prelude_kernel, held_halves, experts, ep_count, tp_count),
        out_shape=pltpu.VMEM((peers, own_rows, part_width + META), jnp.bfloat16),
        in_specs=[pl.BlockSpec(memory_space=pltpu.HBM)] * len(given),
        out_specs=vmem,
        scratch_shapes=[pltpu.VMEM(array.shape, array.dtype) for array in given]
        + [pltpu.SemaphoreType.DMA((len(given),))],
        compiler_params=pltpu.CompilerParams(vmem_limit_bytes=2 * MIB),
        name="prelude",
    )(*[pltpu.with_memory_space_constraint(array, pltpu.HBM) for array in given])
    outgoing = pl.pallas_call(
        pass_kernel,
        out_shape=pltpu.VMEM(outgoing.shape, outgoing.dtype),
        in_specs=[vmem],
        out_specs=vmem,
        input_output_aliases={0: 0},
        cost_estimate=pl.CostEstimate(flops=1 << 36, bytes_accessed=MIB, transcendentals=0),
        compiler_params=pltpu.CompilerParams(vmem_limit_bytes=MIB),
        name="pass_on",
    )(pltpu.with_memory_space_constraint(outgoing, pltpu.VMEM))
    received = lax.all_to_all(outgoing, ("ep", "tp"), split_axis=0, concat_axis=0, tiled=True)
    in_vmem, in_hbm = (
        functools.partial(pltpu.with_memory_space_constraint, memory_space=space)
        for space in (pltpu.VMEM, pltpu.HBM)
    )
    hbm = pl.BlockSpec(memory_space=pltpu.HBM)

    def brought(count):
        shapes = [pltpu.VMEM((count,) + w_down.shape[1:], w_down.dtype)] if count else []
        return shapes, [pltpu.SemaphoreType.DMA((count,))] if count else []

    counts = [held_halves * share // 16 for share in DOWN_SHARES]
    shapes, sems = brought(counts[0])
    gate_part, spread, inputs, *first_down = pl.pallas_call(
        functools.partial(gate_kernel, tp_count, top_count, slots),
        out_shape=[
            pltpu.VMEM((lines, half_ff), jnp.float32),
            pltpu.VMEM((lines, all_rows), jnp.bfloat16),
            pltpu.VMEM((lines, part_width), jnp.bfloat16),
        ]
        + shapes,
        in_specs=[vmem, vmem, hbm],
        out_specs=[vmem] * (3 + len(shapes)),
        scratch_shapes=sems,
        compiler_params=pltpu.CompilerParams(vmem_limit_bytes=2 * MIB),
        name="gate",
    )(received, in_vmem(w_gate), in_hbm(w_down))
    shapes, sems = brought(counts[1])
    up_part, to_send, *next_down = pl.pallas_call(
        functools.partial(up_kernel, slots, counts[0]),
        out_shape=[
            pltpu.VMEM((lines, half_ff), jnp.float32),
            pltpu.VMEM((2, lines, half_ff), jnp.bfloat16),
        ]
        + shapes,
        in_specs=[vmem, vmem, vmem, hbm],
        out_specs=[vmem] * (2 + len(shapes)),
        scratch_shapes=sems,
        compiler_params=pltpu.CompilerParams(vmem_limit_bytes=2 * MIB),
        name="up",
    )(in_vmem(inputs), in_vmem(gate_part), in_vmem(w_up), in_hbm(w_down))
    other = lax.ppermute(to_send, "tp", [(i, i ^ 1) for i in range(tp_count)])
    shapes, sems = brought(counts[2])
    last_down = []
    if shapes:
        last_down = pl.pallas_call(
            functools.partial(bring_kernel, counts[0] + counts[1]),
            out_shape=shapes,
            in_specs=[vmem, hbm],
            out_specs=[vmem],
            scratch_shapes=sems,
            compiler_params=pltpu.CompilerParams(vmem_limit_bytes=MIB),
            name="bring",
        )(in_vmem(up_part), in_hbm(w_down))
    brought_down = [in_vmem(array) for array in (*first_down, *next_down, *last_down)]
    rest = held_halves - sum(counts)
    combined = pl.pallas_call(
        functools.partial(down_kernel, slots),
        out_shape=jax.ShapeDtypeStruct((peers, own_rows, part_width), jnp.bfloat16),
        in_specs=[vmem] * 5 + [hbm] + [vmem] * len(brought_down),
        out_specs=vmem,
        scratch_shapes=[
            pltpu.VMEM((lines, part_width), jnp.bfloat16),
            pltpu.VMEM((rest,) + w_down.shape[1:], w_down.dtype),
            pltpu.SemaphoreType.DMA((rest,)),
        ],
        compiler_params=pltpu.CompilerParams(vmem_limit_bytes=(2 + 3 * (rest + 1) // 2) * MIB),
        name="down",
    )(
        in_vmem(gate_part),
        in_vmem(up_part),
        other,
        unit_scales,
        in_vmem(spread),
        in_hbm(w_down),
        *brought_down,
    )
    returned = lax.all_to_all(
        combined,
        ("ep", "tp"),
        split_axis=0,
        concat_axis=0,
        tiled=True,
    )
    return pl.pallas_call(
        functools.partial(finish_kernel, ep_count),
        out_shape=jax.ShapeDtypeStruct((own_rows, width), jnp.bfloat16),
        in_specs=[vmem],
        out_specs=vmem,
        compiler_params=pltpu.CompilerParams(vmem_limit_bytes=16 * MIB),
        name="finish",
    )(returned)


def solution(mesh):
    placed = (
        P(("groups", "ep", "tp"), None),
        P(),
        P(),
        P(),
        P(("groups", "ep"), None),
        P(("groups", "ep"), None),
        P("ep", "tp", None),
        P("ep", "tp", None),
        P("ep", None, "tp"),
        P("ep", None, None),
    )
    return jax.shard_map(
        body, mesh=mesh, in_specs=placed, out_specs=P(("groups", "ep", "tp"), None), check_vma=False
    )
```

```python
import functools

import jax
import jax.numpy as jnp
from jax import lax
from jax.experimental import pallas as pl
from jax.experimental.pallas import tpu as pltpu
from jax.sharding import PartitionSpec as P

LANES = 128
META = 128
MIB = 1 << 20
DOWN_SHARES = (5, 6, 1)


def terms(value):
    high = value.astype(jnp.bfloat16)
    return high, (value - high.astype(jnp.float32)).astype(jnp.bfloat16)


def dot(left, right, contract=0):
    return lax.dot_general(
        left, right, (((1,), (contract,)), ((), ())), preferred_element_type=jnp.float32
    )


def prelude_kernel(held_halves, experts, ep_count, tp_count, *refs):
    given, out, held, sems = refs[:6], refs[6], refs[7:13], refs[13]
    copies = [pltpu.make_async_copy(a, b, sems.at[i]) for i, (a, b) in enumerate(zip(given, held))]
    for copy in copies:
        copy.start()
    for copy in copies:
        copy.wait()
    hidden, norm_gain, rot_left, rot_right, ids, weights = held
    own_rows, width = hidden.shape
    factor = rot_left.shape[0]
    tiles = width // LANES
    pack = LANES // factor
    top_count = ids.shape[1]
    values = hidden[...].astype(jnp.float32)
    mean_square = jnp.sum(values * values, axis=1, keepdims=True) / width
    normed = values * lax.rsqrt(mean_square + 1e-06) * norm_gain[...]
    lines = jnp.concatenate(
        [normed[:, t * LANES : (t + 1) * LANES] for t in range(tiles)], axis=0
    )
    two = jnp.concatenate([rot_right[...]] * pack, axis=0)
    two = jnp.concatenate([two] * pack, axis=1)
    square = (LANES, LANES)
    line = lax.broadcasted_iota(jnp.int32, square, 0)
    lane = lax.broadcasted_iota(jnp.int32, square, 1)
    two_high, two_low = terms(jnp.where(line // factor == lane // factor, two, 0.0))
    count = tiles * own_rows
    tall = (count, factor)
    tile_of = lax.broadcasted_iota(jnp.int32, tall, 0) // own_rows
    column = lax.broadcasted_iota(jnp.int32, tall, 1)
    picks = [
        jnp.where(column == pack * tile_of + p, 1.0, 0.0).astype(jnp.bfloat16)
        for p in range(pack)
    ]
    same_row = (
        lax.broadcasted_iota(jnp.int32, (pack * count, count), 0) % own_rows
        == lax.broadcasted_iota(jnp.int32, (pack * count, count), 1) % own_rows
    )
    rows_of = jnp.concatenate(picks, axis=0)
    chosen = [dot(rows_of, term).astype(jnp.bfloat16) for term in terms(rot_left[...])]
    blocks = [
        [jnp.where(same_row, dot(term, picks[p], 1), 0.0).astype(jnp.bfloat16) for term in chosen]
        for p in range(pack)
    ]
    high, low = terms(lines)
    lines = dot(high, two_high, 1) + (dot(high, two_low, 1) + dot(low, two_high, 1))
    high, low = terms(lines)
    turned = jnp.zeros((count, LANES), jnp.float32)
    for p_in in range(pack):
        block_high, block_low = blocks[p_in]
        values = dot(block_high, high) + (dot(block_high, low) + dot(block_low, high))
        for p_out in range(pack):
            value = values[p_out * count : (p_out + 1) * count, :]
            shift = ((p_out - p_in) * factor) % LANES
            if shift:
                value = pltpu.roll(value, shift, 1)
            turned = turned + jnp.where(
                lax.broadcasted_iota(jnp.int32, (count, LANES), 1) // factor == p_out, value, 0.0
            )
    rotated = jnp.concatenate(
        [turned[t * own_rows : (t + 1) * own_rows, :] for t in range(tiles)], axis=1
    ).astype(jnp.bfloat16)

    gate_weights = weights[...]
    share = (gate_weights / jnp.sum(gate_weights, axis=1, keepdims=True)).astype(jnp.bfloat16)
    both = jnp.concatenate((ids[...].astype(jnp.float32), share.astype(jnp.float32)), axis=1)
    meta = jnp.concatenate(
        [both[t * own_rows : (t + 1) * own_rows, :] for t in range(tp_count)]
        + [jnp.zeros((own_rows, META - 2 * top_count * tp_count), jnp.float32)],
        axis=1,
    )
    spot = lax.broadcasted_iota(jnp.int32, meta.shape, 1) == META - 1
    part_width = width // tp_count
    for e in range(ep_count):
        first = float(e * held_halves % experts)
        tail = jnp.where(spot, first, meta).astype(jnp.bfloat16)
        for t in range(tp_count):
            out[e * tp_count + t, :, :part_width] = rotated[
                :, t * part_width : (t + 1) * part_width
            ]
            out[e * tp_count + t, :, part_width:] = tail


def bring(w_down, first, held, sems):
    copies = [
        pltpu.make_async_copy(w_down.at[first + i], held.at[i], sems.at[i])
        for i in range(held.shape[0])
    ]

    def start(i, carry):
        pltpu.make_async_copy(w_down.at[first + i], held.at[i], sems.at[i]).start()
        return carry

    lax.fori_loop(0, len(copies), start, 0)
    return copies


def gate_kernel(tp_count, top_count, slots, received_ref, w_gate, w_down, part, spread, inputs, *more):
    held_halves, part_width, half_ff = w_gate.shape
    copies = bring(w_down, 0, *more) if more else []
    peers, own_rows, _ = received_ref.shape
    all_rows = peers * own_rows
    received = received_ref[...].reshape(all_rows, part_width + META)
    meta = received[:, part_width:].astype(jnp.float32).T
    shape = (held_halves, all_rows)
    held = lax.broadcasted_iota(jnp.int32, shape, 0).astype(jnp.float32) + meta[META - 1 :, :]
    group = 2 * top_count
    sender = lax.broadcasted_iota(jnp.int32, (group, all_rows), 1) // own_rows % tp_count
    chosen = meta[:group, :]
    for t in range(1, tp_count):
        chosen = jnp.where(sender == t, meta[t * group : (t + 1) * group, :], chosen)
    member = jnp.zeros(shape, jnp.float32)
    weight = jnp.zeros(shape, jnp.float32)
    for choice in range(top_count):
        named = chosen[choice : choice + 1, :] == held
        member = jnp.where(named, 1.0, member)
        weight = jnp.where(named, chosen[top_count + choice : top_count + choice + 1, :], weight)
    square = (all_rows, all_rows)
    earlier = lax.broadcasted_iota(jnp.int32, square, 0) < lax.broadcasted_iota(
        jnp.int32, square, 1
    )
    rank = jnp.dot(
        member.astype(jnp.bfloat16),
        jnp.where(earlier, 1.0, 0.0).astype(jnp.bfloat16),
        preferred_element_type=jnp.float32,
    )
    rank = jnp.where(member > 0, rank, -1.0)
    slot_index = lax.broadcasted_iota(jnp.int32, (slots, all_rows), 0).astype(jnp.float32)
    selects = []
    for j in range(held_halves):
        selects.append(jnp.where(rank[j : j + 1, :] == slot_index, 1.0, 0.0))
    select = jnp.concatenate(selects, axis=0).astype(jnp.bfloat16)
    inputs[...] = jnp.dot(
        select, received[:, :part_width], preferred_element_type=jnp.float32
    ).astype(jnp.bfloat16)
    for j in range(held_halves):
        window = slice(j * slots, (j + 1) * slots)
        part[window, :] = jnp.dot(
            inputs[window, :], w_gate[j], preferred_element_type=jnp.float32
        )
    for j in range(held_halves):
        spread[j * slots : (j + 1) * slots, :] = jnp.where(
            rank[j : j + 1, :] == slot_index, weight[j : j + 1, :], 0.0
        ).astype(jnp.bfloat16)
    for copy in copies:
        copy.wait()


def up_kernel(slots, first, inputs, gate_part, w_up, w_down, part, to_send, *more):
    copies = bring(w_down, first, *more) if more else []
    for j in range(w_up.shape[0]):
        window = slice(j * slots, (j + 1) * slots)
        value = jnp.dot(inputs[window, :], w_up[j], preferred_element_type=jnp.float32)
        part[window, :] = value
        to_send[0, window, :] = gate_part[window, :].astype(jnp.bfloat16)
        to_send[1, window, :] = value.astype(jnp.bfloat16)
    for copy in copies:
        copy.wait()


def bring_kernel(first, after, w_down, *more):
    del after
    for copy in bring(w_down, first, *more):
        copy.wait()


def down_kernel(slots, gate_part, up_part, other, unit_scales, spread, w_down, *more):
    *brought, out, lines, rest, sems = more
    first = sum(held.shape[0] for held in brought)
    copies = bring(w_down, first, rest, sems)
    held = [ref.at[i] for ref in (*brought, rest) for i in range(ref.shape[0])]
    all_units = []
    for j in range(w_down.shape[0]):
        window = slice(j * slots, (j + 1) * slots)
        gate = (gate_part[window, :] + other[0, window, :].astype(jnp.float32)) * unit_scales[
            j, 0:1, :
        ]
        up = (up_part[window, :] + other[1, window, :].astype(jnp.float32)) * unit_scales[
            j, 1:2, :
        ]
        all_units.append((gate / (1.0 + jnp.exp(-gate)) * up).astype(jnp.bfloat16))
    for j in range(w_down.shape[0]):
        if j == first:
            for copy in copies:
                copy.wait()
        lines[j * slots : (j + 1) * slots, :] = jnp.dot(
            all_units[j], held[j][...], preferred_element_type=jnp.float32
        ).astype(jnp.bfloat16)
    total = lax.dot_general(
        spread[...], lines[...], (((0,), (0,)), ((), ())), preferred_element_type=jnp.float32
    ).astype(jnp.bfloat16)
    out[...] = total.reshape(out.shape)


def finish_kernel(ep_count, returned, out):
    tp_count = returned.shape[0] // ep_count
    part_width = returned.shape[2]
    for t in range(tp_count):
        total = returned[t].astype(jnp.float32)
        for e in range(1, ep_count):
            total = total + returned[e * tp_count + t].astype(jnp.float32)
        out[:, t * part_width : (t + 1) * part_width] = total.astype(jnp.bfloat16)


def body(
    hidden,
    norm_gain,
    rot_left,
    rot_right,
    expert_ids,
    gate_weights,
    w_gate,
    w_up,
    w_down,
    unit_scales,
):
    ep_count = lax.axis_size("ep")
    tp_count = lax.axis_size("tp")
    peers = ep_count * tp_count
    own_rows, width = hidden.shape
    part_width = width // tp_count
    group_rows, top_count = expert_ids.shape
    held_halves, _, half_ff = w_gate.shape
    experts = held_halves * ep_count // 2
    capacity = 5 * group_rows * top_count // (2 * experts)
    slots = capacity * ep_count
    all_rows = peers * own_rows
    lines = held_halves * slots

    vmem = pl.BlockSpec(memory_space=pltpu.VMEM)
    given = (hidden, norm_gain[None, :], rot_left, rot_right, expert_ids, gate_weights)
    outgoing = pl.pallas_call(
        functools.partial(prelude_kernel, held_halves, experts, ep_count, tp_count),
        out_shape=pltpu.VMEM((peers, own_rows, part_width + META), jnp.bfloat16),
        in_specs=[pl.BlockSpec(memory_space=pltpu.HBM)] * len(given),
        out_specs=vmem,
        scratch_shapes=[pltpu.VMEM(array.shape, array.dtype) for array in given]
        + [pltpu.SemaphoreType.DMA((len(given),))],
        cost_estimate=pl.CostEstimate(flops=1 << 36, bytes_accessed=MIB, transcendentals=0),
        compiler_params=pltpu.CompilerParams(vmem_limit_bytes=2 * MIB),
        name="prelude",
    )(*[pltpu.with_memory_space_constraint(array, pltpu.HBM) for array in given])
    received = lax.all_to_all(outgoing, ("ep", "tp"), split_axis=0, concat_axis=0, tiled=True)
    in_vmem, in_hbm = (
        functools.partial(pltpu.with_memory_space_constraint, memory_space=space)
        for space in (pltpu.VMEM, pltpu.HBM)
    )
    hbm = pl.BlockSpec(memory_space=pltpu.HBM)

    def brought(count):
        shapes = [pltpu.VMEM((count,) + w_down.shape[1:], w_down.dtype)] if count else []
        return shapes, [pltpu.SemaphoreType.DMA((count,))] if count else []

    counts = [held_halves * share // 16 for share in DOWN_SHARES]
    shapes, sems = brought(counts[0])
    gate_part, spread, inputs, *first_down = pl.pallas_call(
        functools.partial(gate_kernel, tp_count, top_count, slots),
        out_shape=[
            pltpu.VMEM((lines, half_ff), jnp.float32),
            pltpu.VMEM((lines, all_rows), jnp.bfloat16),
            pltpu.VMEM((lines, part_width), jnp.bfloat16),
        ]
        + shapes,
        in_specs=[vmem, vmem, hbm],
        out_specs=[vmem] * (3 + len(shapes)),
        scratch_shapes=sems,
        compiler_params=pltpu.CompilerParams(vmem_limit_bytes=2 * MIB),
        name="gate",
    )(received, in_vmem(w_gate), in_hbm(w_down))
    shapes, sems = brought(counts[1])
    up_part, to_send, *next_down = pl.pallas_call(
        functools.partial(up_kernel, slots, counts[0]),
        out_shape=[
            pltpu.VMEM((lines, half_ff), jnp.float32),
            pltpu.VMEM((2, lines, half_ff), jnp.bfloat16),
        ]
        + shapes,
        in_specs=[vmem, vmem, vmem, hbm],
        out_specs=[vmem] * (2 + len(shapes)),
        scratch_shapes=sems,
        compiler_params=pltpu.CompilerParams(vmem_limit_bytes=2 * MIB),
        name="up",
    )(in_vmem(inputs), in_vmem(gate_part), in_vmem(w_up), in_hbm(w_down))
    other = lax.ppermute(to_send, "tp", [(i, i ^ 1) for i in range(tp_count)])
    shapes, sems = brought(counts[2])
    last_down = []
    if shapes:
        last_down = pl.pallas_call(
            functools.partial(bring_kernel, counts[0] + counts[1]),
            out_shape=shapes,
            in_specs=[vmem, hbm],
            out_specs=[vmem],
            scratch_shapes=sems,
            compiler_params=pltpu.CompilerParams(vmem_limit_bytes=MIB),
            name="bring",
        )(in_vmem(up_part), in_hbm(w_down))
    brought_down = [in_vmem(array) for array in (*first_down, *next_down, *last_down)]
    rest = held_halves - sum(counts)
    combined = pl.pallas_call(
        functools.partial(down_kernel, slots),
        out_shape=jax.ShapeDtypeStruct((peers, own_rows, part_width), jnp.bfloat16),
        in_specs=[vmem] * 5 + [hbm] + [vmem] * len(brought_down),
        out_specs=vmem,
        scratch_shapes=[
            pltpu.VMEM((lines, part_width), jnp.bfloat16),
            pltpu.VMEM((rest,) + w_down.shape[1:], w_down.dtype),
            pltpu.SemaphoreType.DMA((rest,)),
        ],
        compiler_params=pltpu.CompilerParams(vmem_limit_bytes=(2 + 3 * (rest + 1) // 2) * MIB),
        name="down",
    )(
        in_vmem(gate_part),
        in_vmem(up_part),
        other,
        unit_scales,
        in_vmem(spread),
        in_hbm(w_down),
        *brought_down,
    )
    returned = lax.all_to_all(
        combined,
        ("ep", "tp"),
        split_axis=0,
        concat_axis=0,
        tiled=True,
    )
    return pl.pallas_call(
        functools.partial(finish_kernel, ep_count),
        out_shape=jax.ShapeDtypeStruct((own_rows, width), jnp.bfloat16),
        in_specs=[vmem],
        out_specs=vmem,
        compiler_params=pltpu.CompilerParams(vmem_limit_bytes=16 * MIB),
        name="finish",
    )(returned)


def solution(mesh):
    placed = (
        P(("groups", "ep", "tp"), None),
        P(),
        P(),
        P(),
        P(("groups", "ep"), None),
        P(("groups", "ep"), None),
        P("ep", "tp", None),
        P("ep", "tp", None),
        P("ep", None, "tp"),
        P("ep", None, None),
    )
    return jax.shard_map(
        body, mesh=mesh, in_specs=placed, out_specs=P(("groups", "ep", "tp"), None), check_vma=False
    )
```

```python
import functools

import jax
import jax.numpy as jnp
from jax import lax
from jax.experimental import pallas as pl
from jax.experimental.pallas import tpu as pltpu
from jax.sharding import PartitionSpec as P

LANES = 128
META = 128
MIB = 1 << 20
DOWN_SHARES = (5, 6, 1)


def terms(value):
    high = value.astype(jnp.bfloat16)
    return high, (value - high.astype(jnp.float32)).astype(jnp.bfloat16)


def dot(left, right, contract=0):
    return lax.dot_general(
        left, right, (((1,), (contract,)), ((), ())), preferred_element_type=jnp.float32
    )


def prelude_kernel(held_halves, experts, ep_count, tp_count, *refs):
    given, out, held, sems = refs[:6], refs[6], refs[7:13], refs[13]
    copies = [pltpu.make_async_copy(a, b, sems.at[i]) for i, (a, b) in enumerate(zip(given, held))]
    for copy in copies:
        copy.start()
    for copy in copies:
        copy.wait()
    hidden, norm_gain, rot_left, rot_right, ids, weights = held
    own_rows, width = hidden.shape
    factor = rot_left.shape[0]
    tiles = width // LANES
    pack = LANES // factor
    top_count = ids.shape[1]
    values = hidden[...].astype(jnp.float32)
    mean_square = jnp.sum(values * values, axis=1, keepdims=True) / width
    normed = values * lax.rsqrt(mean_square + 1e-06) * norm_gain[...]
    lines = jnp.concatenate(
        [normed[:, t * LANES : (t + 1) * LANES] for t in range(tiles)], axis=0
    )
    two = jnp.concatenate([rot_right[...]] * pack, axis=0)
    two = jnp.concatenate([two] * pack, axis=1)
    square = (LANES, LANES)
    line = lax.broadcasted_iota(jnp.int32, square, 0)
    lane = lax.broadcasted_iota(jnp.int32, square, 1)
    two_high, two_low = terms(jnp.where(line // factor == lane // factor, two, 0.0))
    count = tiles * own_rows
    tall = (count, factor)
    tile_of = lax.broadcasted_iota(jnp.int32, tall, 0) // own_rows
    column = lax.broadcasted_iota(jnp.int32, tall, 1)
    picks = [
        jnp.where(column == pack * tile_of + p, 1.0, 0.0).astype(jnp.bfloat16)
        for p in range(pack)
    ]
    same_row = (
        lax.broadcasted_iota(jnp.int32, (pack * count, count), 0) % own_rows
        == lax.broadcasted_iota(jnp.int32, (pack * count, count), 1) % own_rows
    )
    rows_of = jnp.concatenate(picks, axis=0)
    chosen = [dot(rows_of, term).astype(jnp.bfloat16) for term in terms(rot_left[...])]
    blocks = [
        [jnp.where(same_row, dot(term, picks[p], 1), 0.0).astype(jnp.bfloat16) for term in chosen]
        for p in range(pack)
    ]
    high, low = terms(lines)
    lines = dot(high, two_high, 1) + (dot(high, two_low, 1) + dot(low, two_high, 1))
    high, low = terms(lines)
    turned = jnp.zeros((count, LANES), jnp.float32)
    for p_in in range(pack):
        block_high, block_low = blocks[p_in]
        values = dot(block_high, high) + (dot(block_high, low) + dot(block_low, high))
        for p_out in range(pack):
            value = values[p_out * count : (p_out + 1) * count, :]
            shift = ((p_out - p_in) * factor) % LANES
            if shift:
                value = pltpu.roll(value, shift, 1)
            turned = turned + jnp.where(
                lax.broadcasted_iota(jnp.int32, (count, LANES), 1) // factor == p_out, value, 0.0
            )
    rotated = jnp.concatenate(
        [turned[t * own_rows : (t + 1) * own_rows, :] for t in range(tiles)], axis=1
    ).astype(jnp.bfloat16)

    gate_weights = weights[...]
    share = (gate_weights / jnp.sum(gate_weights, axis=1, keepdims=True)).astype(jnp.bfloat16)
    both = jnp.concatenate((ids[...].astype(jnp.float32), share.astype(jnp.float32)), axis=1)
    meta = jnp.concatenate(
        [both[t * own_rows : (t + 1) * own_rows, :] for t in range(tp_count)]
        + [jnp.zeros((own_rows, META - 2 * top_count * tp_count), jnp.float32)],
        axis=1,
    )
    spot = lax.broadcasted_iota(jnp.int32, meta.shape, 1) == META - 1
    part_width = width // tp_count
    for e in range(ep_count):
        first = float(e * held_halves % experts)
        tail = jnp.where(spot, first, meta).astype(jnp.bfloat16)
        for t in range(tp_count):
            out[e * tp_count + t, :, :part_width] = rotated[
                :, t * part_width : (t + 1) * part_width
            ]
            out[e * tp_count + t, :, part_width:] = tail


def bring(w_down, first, held, sems):
    copies = [
        pltpu.make_async_copy(w_down.at[first + i], held.at[i], sems.at[i])
        for i in range(held.shape[0])
    ]

    def start(i, carry):
        pltpu.make_async_copy(w_down.at[first + i], held.at[i], sems.at[i]).start()
        return carry

    lax.fori_loop(0, len(copies), start, 0)
    return copies


def gate_kernel(tp_count, top_count, slots, received_ref, w_gate, w_down, part, spread, inputs, *more):
    held_halves, part_width, half_ff = w_gate.shape
    copies = bring(w_down, 0, *more) if more else []
    peers, own_rows, _ = received_ref.shape
    all_rows = peers * own_rows
    received = received_ref[...].reshape(all_rows, part_width + META)
    meta = received[:, part_width:].astype(jnp.float32).T
    shape = (held_halves, all_rows)
    held = lax.broadcasted_iota(jnp.int32, shape, 0).astype(jnp.float32) + meta[META - 1 :, :]
    group = 2 * top_count
    sender = lax.broadcasted_iota(jnp.int32, (group, all_rows), 1) // own_rows % tp_count
    chosen = meta[:group, :]
    for t in range(1, tp_count):
        chosen = jnp.where(sender == t, meta[t * group : (t + 1) * group, :], chosen)
    member = jnp.zeros(shape, jnp.float32)
    weight = jnp.zeros(shape, jnp.float32)
    for choice in range(top_count):
        named = chosen[choice : choice + 1, :] == held
        member = jnp.where(named, 1.0, member)
        weight = jnp.where(named, chosen[top_count + choice : top_count + choice + 1, :], weight)
    square = (all_rows, all_rows)
    earlier = lax.broadcasted_iota(jnp.int32, square, 0) < lax.broadcasted_iota(
        jnp.int32, square, 1
    )
    rank = jnp.dot(
        member.astype(jnp.bfloat16),
        jnp.where(earlier, 1.0, 0.0).astype(jnp.bfloat16),
        preferred_element_type=jnp.float32,
    )
    rank = jnp.where(member > 0, rank, -1.0)
    slot_index = lax.broadcasted_iota(jnp.int32, (slots, all_rows), 0).astype(jnp.float32)
    selects = []
    for j in range(held_halves):
        select = rank[j : j + 1, :] == slot_index
        selects.append(jnp.where(select, 1.0, 0.0))
        spread[j * slots : (j + 1) * slots, :] = jnp.where(
            select, weight[j : j + 1, :], 0.0
        ).astype(jnp.bfloat16)
    select = jnp.concatenate(selects, axis=0).astype(jnp.bfloat16)
    inputs[...] = jnp.dot(
        select, received[:, :part_width], preferred_element_type=jnp.float32
    ).astype(jnp.bfloat16)
    for j in range(held_halves):
        window = slice(j * slots, (j + 1) * slots)
        part[window, :] = jnp.dot(
            inputs[window, :], w_gate[j], preferred_element_type=jnp.float32
        )
    for copy in copies:
        copy.wait()


def up_kernel(slots, first, inputs, gate_part, w_up, w_down, part, to_send, *more):
    copies = bring(w_down, first, *more) if more else []
    for j in range(w_up.shape[0]):
        window = slice(j * slots, (j + 1) * slots)
        value = jnp.dot(inputs[window, :], w_up[j], preferred_element_type=jnp.float32)
        part[window, :] = value
        to_send[0, window, :] = gate_part[window, :].astype(jnp.bfloat16)
        to_send[1, window, :] = value.astype(jnp.bfloat16)
    for copy in copies:
        copy.wait()


def bring_kernel(first, after, w_down, *more):
    del after
    for copy in bring(w_down, first, *more):
        copy.wait()


def down_kernel(slots, gate_part, up_part, other, unit_scales, spread, w_down, *more):
    *brought, out, lines, rest, sems = more
    first = sum(held.shape[0] for held in brought)
    copies = bring(w_down, first, rest, sems)
    held = [ref.at[i] for ref in (*brought, rest) for i in range(ref.shape[0])]
    all_units = []
    for j in range(w_down.shape[0]):
        window = slice(j * slots, (j + 1) * slots)
        gate = (gate_part[window, :] + other[0, window, :].astype(jnp.float32)) * unit_scales[
            j, 0:1, :
        ]
        up = (up_part[window, :] + other[1, window, :].astype(jnp.float32)) * unit_scales[
            j, 1:2, :
        ]
        all_units.append((gate / (1.0 + jnp.exp(-gate)) * up).astype(jnp.bfloat16))
    total = jnp.zeros((spread.shape[1], w_down.shape[2]), jnp.float32)
    for start, end in ((0, first), (first, w_down.shape[0])):
        if start == end:
            continue
        if start == first:
            for copy in copies:
                copy.wait()
        for j in range(start, end):
            lines[j * slots : (j + 1) * slots, :] = jnp.dot(
                all_units[j], held[j][...], preferred_element_type=jnp.float32
            ).astype(jnp.bfloat16)
        window = slice(start * slots, end * slots)
        total = total + lax.dot_general(
            spread[window, :],
            lines[window, :],
            (((0,), (0,)), ((), ())),
            preferred_element_type=jnp.float32,
        )
    total = total.astype(jnp.bfloat16)
    out[...] = total.reshape(out.shape)


def finish_kernel(ep_count, returned, out):
    tp_count = returned.shape[0] // ep_count
    part_width = returned.shape[2]
    for t in range(tp_count):
        total = returned[t].astype(jnp.float32)
        for e in range(1, ep_count):
            total = total + returned[e * tp_count + t].astype(jnp.float32)
        out[:, t * part_width : (t + 1) * part_width] = total.astype(jnp.bfloat16)


def body(
    hidden,
    norm_gain,
    rot_left,
    rot_right,
    expert_ids,
    gate_weights,
    w_gate,
    w_up,
    w_down,
    unit_scales,
):
    ep_count = lax.axis_size("ep")
    tp_count = lax.axis_size("tp")
    peers = ep_count * tp_count
    own_rows, width = hidden.shape
    part_width = width // tp_count
    group_rows, top_count = expert_ids.shape
    held_halves, _, half_ff = w_gate.shape
    experts = held_halves * ep_count // 2
    capacity = 5 * group_rows * top_count // (2 * experts)
    slots = capacity * ep_count
    all_rows = peers * own_rows
    lines = held_halves * slots

    vmem = pl.BlockSpec(memory_space=pltpu.VMEM)
    given = (hidden, norm_gain[None, :], rot_left, rot_right, expert_ids, gate_weights)
    outgoing = pl.pallas_call(
        functools.partial(prelude_kernel, held_halves, experts, ep_count, tp_count),
        out_shape=pltpu.VMEM((peers, own_rows, part_width + META), jnp.bfloat16),
        in_specs=[pl.BlockSpec(memory_space=pltpu.HBM)] * len(given),
        out_specs=vmem,
        scratch_shapes=[pltpu.VMEM(array.shape, array.dtype) for array in given]
        + [pltpu.SemaphoreType.DMA((len(given),))],
        cost_estimate=pl.CostEstimate(flops=1 << 36, bytes_accessed=MIB, transcendentals=0),
        compiler_params=pltpu.CompilerParams(vmem_limit_bytes=2 * MIB),
        name="prelude",
    )(*[pltpu.with_memory_space_constraint(array, pltpu.HBM) for array in given])
    received = lax.all_to_all(outgoing, ("ep", "tp"), split_axis=0, concat_axis=0, tiled=True)
    in_vmem, in_hbm = (
        functools.partial(pltpu.with_memory_space_constraint, memory_space=space)
        for space in (pltpu.VMEM, pltpu.HBM)
    )
    hbm = pl.BlockSpec(memory_space=pltpu.HBM)

    def brought(count):
        shapes = [pltpu.VMEM((count,) + w_down.shape[1:], w_down.dtype)] if count else []
        return shapes, [pltpu.SemaphoreType.DMA((count,))] if count else []

    counts = [held_halves * share // 16 for share in DOWN_SHARES]
    shapes, sems = brought(counts[0])
    gate_part, spread, inputs, *first_down = pl.pallas_call(
        functools.partial(gate_kernel, tp_count, top_count, slots),
        out_shape=[
            pltpu.VMEM((lines, half_ff), jnp.float32),
            pltpu.VMEM((lines, all_rows), jnp.bfloat16),
            pltpu.VMEM((lines, part_width), jnp.bfloat16),
        ]
        + shapes,
        in_specs=[vmem, vmem, hbm],
        out_specs=[vmem] * (3 + len(shapes)),
        scratch_shapes=sems,
        compiler_params=pltpu.CompilerParams(vmem_limit_bytes=2 * MIB),
        name="gate",
    )(received, in_vmem(w_gate), in_hbm(w_down))
    shapes, sems = brought(counts[1])
    up_part, to_send, *next_down = pl.pallas_call(
        functools.partial(up_kernel, slots, counts[0]),
        out_shape=[
            pltpu.VMEM((lines, half_ff), jnp.float32),
            pltpu.VMEM((2, lines, half_ff), jnp.bfloat16),
        ]
        + shapes,
        in_specs=[vmem, vmem, vmem, hbm],
        out_specs=[vmem] * (2 + len(shapes)),
        scratch_shapes=sems,
        compiler_params=pltpu.CompilerParams(vmem_limit_bytes=2 * MIB),
        name="up",
    )(in_vmem(inputs), in_vmem(gate_part), in_vmem(w_up), in_hbm(w_down))
    other = lax.ppermute(to_send, "tp", [(i, i ^ 1) for i in range(tp_count)])
    shapes, sems = brought(counts[2])
    last_down = []
    if shapes:
        last_down = pl.pallas_call(
            functools.partial(bring_kernel, counts[0] + counts[1]),
            out_shape=shapes,
            in_specs=[vmem, hbm],
            out_specs=[vmem],
            scratch_shapes=sems,
            compiler_params=pltpu.CompilerParams(vmem_limit_bytes=MIB),
            name="bring",
        )(in_vmem(up_part), in_hbm(w_down))
    brought_down = [in_vmem(array) for array in (*first_down, *next_down, *last_down)]
    rest = held_halves - sum(counts)
    combined = pl.pallas_call(
        functools.partial(down_kernel, slots),
        out_shape=jax.ShapeDtypeStruct((peers, own_rows, part_width), jnp.bfloat16),
        in_specs=[vmem] * 5 + [hbm] + [vmem] * len(brought_down),
        out_specs=vmem,
        scratch_shapes=[
            pltpu.VMEM((lines, part_width), jnp.bfloat16),
            pltpu.VMEM((rest,) + w_down.shape[1:], w_down.dtype),
            pltpu.SemaphoreType.DMA((rest,)),
        ],
        compiler_params=pltpu.CompilerParams(vmem_limit_bytes=(2 + 3 * (rest + 1) // 2) * MIB),
        name="down",
    )(
        in_vmem(gate_part),
        in_vmem(up_part),
        other,
        unit_scales,
        in_vmem(spread),
        in_hbm(w_down),
        *brought_down,
    )
    returned = lax.all_to_all(
        combined,
        ("ep", "tp"),
        split_axis=0,
        concat_axis=0,
        tiled=True,
    )
    return pl.pallas_call(
        functools.partial(finish_kernel, ep_count),
        out_shape=jax.ShapeDtypeStruct((own_rows, width), jnp.bfloat16),
        in_specs=[vmem],
        out_specs=vmem,
        compiler_params=pltpu.CompilerParams(vmem_limit_bytes=16 * MIB),
        name="finish",
    )(returned)


def solution(mesh):
    placed = (
        P(("groups", "ep", "tp"), None),
        P(),
        P(),
        P(),
        P(("groups", "ep"), None),
        P(("groups", "ep"), None),
        P("ep", "tp", None),
        P("ep", "tp", None),
        P("ep", None, "tp"),
        P("ep", None, None),
    )
    return jax.shard_map(
        body, mesh=mesh, in_specs=placed, out_specs=P(("groups", "ep", "tp"), None), check_vma=False
    )
```
